512 devices in a mesh: rep: 64 (over x_lo, z, core), tp: 8 (over y, x_hi).
Axes of the slice: x: 4 (x_hi: 2, x_lo: 2; x = x_hi * 2 + x_lo), y: 4, z: 16, core: 2. Of those that a mesh axis runs over, the one named last changes fastest.
Arguments:
- prompt_q: bfloat16 [32768, 2048], P('rep', 'tp'), may hold values from -24 to 24
- prompt_k: bfloat16 [32768, 2048], P('rep', 'tp'), may hold values from -24 to 24
- prompt_v: bfloat16 [32768, 2048], P('rep', 'tp'), may hold values from -6 to 6
- prompt_len: int32 [64], P('rep'), may hold values from 256 to 512, as said below
- cache_keys: bfloat16 [128, 1024, 2048], P('rep', None, 'tp'), may hold values from -24 to 24
- cache_values: bfloat16 [128, 1024, 2048], P('rep', None, 'tp'), may hold values from -6 to 6
- new_q: bfloat16 [128, 2048], P('rep', 'tp'), may hold values from -24 to 24
- new_k: bfloat16 [128, 2048], P('rep', 'tp'), may hold values from -6 to 6
- new_v: bfloat16 [128, 2048], P('rep', 'tp'), may hold values from -6 to 6
- cache_len: int32 [128], replicated, may hold values from 260 to 1024, as said below
- moving: int32 [64], replicated, may hold values from 0 to 1
- out_weight: bfloat16 [2048, 2048], P(None, 'tp'), may hold values from -0.125 to 0.125
- out_bias: float32 [2048], P('tp'), may hold values from -1.75 to 1.75
- residual: bfloat16 [32896, 2048], P('rep', 'tp'), may hold values from -150 to 150
- ln_gain: float32 [2048], P('tp'), may hold values from 0.1 to 1.9
- ln_shift: float32 [2048], P('tp'), may hold values from -1.75 to 1.75
Outputs:
- hidden_out: bfloat16 [32896, 2048], P('rep', 'tp')
- normed: bfloat16 [32896, 2048], P('rep', 'tp')
- moved_window: bfloat16 [64, 2, 260, 2048], P('rep', None, None, 'tp')
The draws below stay inside these ranges and needn't reach their ends.
Inputs may be any that keep to these rules, and one draw needn't show every extreme that they name: `prompt_len`: some replica's prompt has all 512 tokens live. `cache_len`: some request's cache is full.
All inputs are finite; a program needn't handle non-finite values.
Results may differ from the reference program's by a relative error of at most 0.0022.
Values may be sent and summed in bfloat16 or wider, within the bound.
No kernel may reach another device: no remote copies, remote signals or barrier semaphores. Data moves between devices by JAX's collectives and lax.ppermute only.
A program may use at most 64 MiB of HBM per device.

```python
import math
import jax
import jax.numpy as jnp
from jax import lax

D = 2048
HEADS = 16
HD = 128
PL = 512
SLOTS = 2
CAP = 1024
SINK = 4
WIN = 256
SPAN = 260
REPLICAS = 64
TOKENS = 32768
REQUESTS = 128
ROWS = 32896


def drawn_draw(key, shape):
    return jax.random.truncated_normal(key, -6.0, 6.0, shape, jnp.float32)


def draw_prompt_q(key, part):
    base_draw = drawn_draw(jax.random.fold_in(key, 1), (TOKENS, D))
    return base_draw.astype(jnp.bfloat16)


def draw_prompt_k(key, part):
    base_draw = drawn_draw(jax.random.fold_in(key, 2), (TOKENS, D))
    return base_draw.astype(jnp.bfloat16)


def draw_new_q(key, part):
    base_draw = drawn_draw(jax.random.fold_in(key, 3), (REQUESTS, D))
    return base_draw.astype(jnp.bfloat16)


def draw_cache_keys(key, part):
    base_draw = drawn_draw(jax.random.fold_in(key, 4), (REQUESTS, CAP, D))
    return base_draw.astype(jnp.bfloat16)


def draw_cache_len(key, part):
    lengths = jax.random.randint(jax.random.fold_in(key, 5), (REQUESTS,), SINK + WIN, CAP + 1, jnp.int32)
    chosen = jax.random.randint(jax.random.fold_in(key, 6), (), 0, REQUESTS, jnp.int32)
    return jnp.where(jnp.arange(REQUESTS, dtype=jnp.int32) == chosen, CAP, lengths).astype(jnp.int32)


def draw_prompt_len(key, part):
    lengths = jax.random.randint(jax.random.fold_in(key, 7), (REPLICAS,), PL // 2, PL + 1, jnp.int32)
    chosen = jax.random.randint(jax.random.fold_in(key, 8), (), 0, REPLICAS, jnp.int32)
    return jnp.where(jnp.arange(REPLICAS, dtype=jnp.int32) == chosen, PL, lengths).astype(jnp.int32)


def draw_residual(key, part):
    column = jnp.arange(D, dtype=jnp.float32)
    ramp = jnp.exp(jnp.log(3.0) * column / D)
    column_scale = 0.3 * jnp.exp(jnp.log(10.0) * jax.random.uniform(jax.random.fold_in(key, 21), (D,), jnp.float32))
    base_draw = jax.random.truncated_normal(jax.random.fold_in(key, 25), -6.0, 6.0, (ROWS, D), jnp.float32)
    values = base_draw * (column_scale * ramp)[None, :]
    return values.astype(jnp.bfloat16)


def set_ends(drawn, key, least, largest):
    place = [jax.random.randint(jax.random.fold_in(key, axis), (), 0, length) for axis, length in enumerate(drawn.shape)]
    main_axis = drawn.shape.index(max(drawn.shape))
    next_to = place[:main_axis] + [(place[main_axis] + 1) % drawn.shape[main_axis]] + place[main_axis + 1:]
    return drawn.at[tuple(place)].set(least).at[tuple(next_to)].set(largest)


def block_levels(rng, dims, pieces, least, high):
    def one(dim, blocks):
        steps = jax.random.uniform(jax.random.fold_in(jax.random.fold_in(rng, 6), dim), (blocks,), jnp.float32, least / len(pieces), high / len(pieces))
        return jnp.repeat(jnp.exp(steps), dims[dim] // blocks).reshape((-1,) + (1,) * (len(dims) - dim - 1))

    gain = one(*pieces[0])
    for cut in pieces[1:]:
        gain = gain * one(*cut)
    return gain


def scatter_about(key, extent, width, most, cuts=(), held_as=jnp.bfloat16):
    values = width * jax.random.normal(key, extent, jnp.float32)
    if cuts:
        values = values * block_levels(key, extent, cuts, -0.22, 0.18)
    return jnp.clip(values, -most, most).astype(held_as)


def setup_inputs(seed: int = 0) -> dict:
    key_list = jax.random.split(jax.random.key(seed), 17)
    prompt_q = draw_prompt_q(jax.random.fold_in(key_list[16], 71), 0)
    prompt_k = draw_prompt_k(jax.random.fold_in(key_list[16], 71), 0)
    prompt_v = scatter_about(key_list[2], (TOKENS, D), 1.0, 6.0, ((0, 64), (1, 8)))
    prompt_len = draw_prompt_len(jax.random.fold_in(key_list[16], 71), 0)
    cache_keys = draw_cache_keys(jax.random.fold_in(key_list[16], 71), 0)
    cache_values = scatter_about(key_list[5], (REQUESTS, CAP, D), 1.0, 6.0, ((0, 64), (2, 8)))
    new_q = draw_new_q(jax.random.fold_in(key_list[16], 71), 0)
    new_k = scatter_about(key_list[7], (REQUESTS, D), 1.0, 6.0, ((0, 64), (1, 8)))
    new_v = scatter_about(key_list[8], (REQUESTS, D), 1.0, 6.0, ((0, 64), (1, 8)))
    cache_len = draw_cache_len(jax.random.fold_in(key_list[16], 71), 0)
    moving = set_ends(jax.random.randint(key_list[10], (REPLICAS,), 0, SLOTS), jax.random.fold_in(key_list[10], 1), 0, SLOTS - 1).astype(jnp.int32)
    out_weight = scatter_about(key_list[11], (D, D), D ** -0.5, 0.125, ((1, 8),))
    out_bias = scatter_about(key_list[12], (D,), 0.3, 1.75, ((0, 8),), jnp.float32)
    residual = draw_residual(jax.random.fold_in(key_list[16], 71), 0)
    ln_gain = jnp.clip(1.0 + 0.18 * jax.random.normal(key_list[14], (D,), jnp.float32), 0.1, 1.9)
    ln_shift = scatter_about(key_list[15], (D,), 0.3, 1.75, ((0, 8),), jnp.float32)
    return {"prompt_q": prompt_q, "prompt_k": prompt_k, "prompt_v": prompt_v, "prompt_len": prompt_len, "cache_keys": cache_keys, "cache_values": cache_values, "new_q": new_q, "new_k": new_k, "new_v": new_v, "cache_len": cache_len, "moving": moving, "out_weight": out_weight, "out_bias": out_bias, "residual": residual, "ln_gain": ln_gain, "ln_shift": ln_shift}


masked_score = -1e+30
norm_epsilon = 1e-05

def all_slopes():
    head_ids = jnp.arange(HEADS, dtype=jnp.float32)
    return jnp.exp2(-8.0 * (head_ids + 1.0) / HEADS)

def softmax_rows(scores):
    row_max = lax.optimization_barrier(jnp.max(scores, axis=-1, keepdims=True))
    expo_terms = jnp.exp(scores - row_max)
    return (expo_terms / lax.optimization_barrier(jnp.sum(expo_terms, axis=-1, keepdims=True))).astype(jnp.bfloat16)

def prompt_attend(packed):
    query_rows, key_rows, value_rows, length = packed
    slopes = all_slopes()
    query_heads = query_rows.astype(jnp.float32).reshape(PL, HEADS, HD)
    key_heads = key_rows.astype(jnp.float32).reshape(PL, HEADS, HD)
    value_heads = value_rows.astype(jnp.float32).reshape(PL, HEADS, HD)
    scores = jnp.einsum('qhd,khd->hqk', query_heads, key_heads) * (1.0 / math.sqrt(HD))
    position = jnp.arange(PL, dtype=jnp.int32)
    distance = (position[:, None] - position[None, :]).astype(jnp.float32)
    scores = scores - slopes[:, None, None] * distance[None]
    allowed = (position[None, :] <= position[:, None]) & (position[None, :] < length)
    scores = jnp.where(allowed[None], scores, masked_score)
    weights = softmax_rows(scores)
    mixed_heads = jnp.einsum('hqk,khd->qhd', weights.astype(jnp.float32), value_heads)
    return mixed_heads.astype(jnp.bfloat16).reshape(PL, D)

def window_rows(cache_rows, newest, length):
    middle = lax.dynamic_slice_in_dim(cache_rows, (length + 1 - WIN).astype(jnp.int32), WIN - 1, 0)
    return jnp.concatenate([cache_rows[:SINK], middle, newest[None]], axis=0)

def window_positions(length):
    sink_part = jnp.arange(SINK, dtype=jnp.int32)
    tail_part = length + 1 - WIN + jnp.arange(WIN, dtype=jnp.int32)
    return jnp.concatenate([sink_part, tail_part])

def reference(prompt_q, prompt_k, prompt_v, prompt_len, cache_keys, cache_values, new_q, new_k, new_v, cache_len, moving, out_weight, out_bias, residual, ln_gain, ln_shift):
    prompt_mix = lax.map(prompt_attend, (prompt_q.reshape(REPLICAS, PL, D), prompt_k.reshape(REPLICAS, PL, D), prompt_v.reshape(REPLICAS, PL, D), prompt_len))
    replica_ids = jnp.arange(REPLICAS, dtype=jnp.int32)
    partner = (replica_ids + REPLICAS // 2) % REPLICAS
    staying = replica_ids * SLOTS + 1 - moving
    arriving = partner * SLOTS + moving[partner]
    served = jnp.stack([staying, arriving], axis=1).reshape(-1).astype(jnp.int32)
    slopes = all_slopes()

    def decode_one(request):
        length = cache_len[request]
        key_window = window_rows(cache_keys[request], new_k[request], length)
        value_window = window_rows(cache_values[request], new_v[request], length)
        query_heads = new_q[request].astype(jnp.float32).reshape(HEADS, HD)
        key_heads = key_window.astype(jnp.float32).reshape(SPAN, HEADS, HD)
        value_heads = value_window.astype(jnp.float32).reshape(SPAN, HEADS, HD)
        scores = jnp.einsum('hd,whd->hw', query_heads, key_heads) * (1.0 / math.sqrt(HD))
        distance = (length - window_positions(length)).astype(jnp.float32)
        scores = scores - slopes[:, None] * distance[None, :]
        weights = softmax_rows(scores)
        mixed_heads = jnp.einsum('hw,whd->hd', weights.astype(jnp.float32), value_heads)
        return (mixed_heads.astype(jnp.bfloat16).reshape(D), key_window, value_window)
    decode_mix, key_windows, value_windows = lax.map(decode_one, served)
    mixed_rows = jnp.concatenate([prompt_mix, decode_mix.reshape(REPLICAS, SLOTS, D)], axis=1).reshape(ROWS, D)
    stream = jnp.dot(mixed_rows, out_weight, preferred_element_type=jnp.float32) + out_bias[None, :] + residual.astype(jnp.float32)
    hidden_out = stream.astype(jnp.bfloat16)
    row_mean = lax.optimization_barrier(jnp.mean(stream, axis=1, keepdims=True))
    centered = stream - row_mean
    row_var = lax.optimization_barrier(jnp.mean(centered * centered, axis=1, keepdims=True))
    normed = (centered * lax.rsqrt(row_var + norm_epsilon) * ln_gain[None, :] + ln_shift[None, :]).astype(jnp.bfloat16)
    moved_keys = key_windows.reshape(REPLICAS, SLOTS, SPAN, D)[:, 1]
    moved_values = value_windows.reshape(REPLICAS, SLOTS, SPAN, D)[:, 1]
    moved_window = jnp.stack([moved_keys, moved_values], axis=1)
    return (hidden_out, normed, moved_window)
```

```python
import functools
import math

import jax
import jax.numpy as jnp
from jax import lax
from jax.experimental import pallas as pl
from jax.experimental.pallas import tpu as pltpu
from jax.sharding import PartitionSpec as P

D = 2048
HEADS = 16
HD = 128
SINK = 4
WIN = 256
SPAN = SINK + WIN
ROW_TILE = 16
COPY = 272

LOG2E = math.log2(math.e)
SCALE = LOG2E / math.sqrt(HD)
MASKED = -1e30
EPSILON = 1e-05

F32 = jnp.float32
BF16 = jnp.bfloat16
HIGHEST = lax.Precision.HIGHEST


def dot(a, b, contract, precision=None):
    return lax.dot_general(a, b, (contract, ((), ())), precision=precision, preferred_element_type=F32)


def head_slope(local_heads, head):
    tp = lax.axis_index("tp")
    slope = jnp.float32(LOG2E * 2.0 ** (-8.0 * (head + 1) / HEADS))
    step = 2.0 ** (-8.0 * local_heads / HEADS)
    for k in range(1, HEADS // local_heads):
        slope = jnp.where(tp >= k, slope * step, slope)
    return slope


def decode_kernel(
    moving, cache_len, new_q, new_k, new_v, cache_k, cache_v,
    window_out, stay_out, leave_out, body, sink, sems,
):
    rep = lax.axis_index("rep")
    slots, capacity, width = cache_k.shape
    local_heads = width // HD
    leaving = moving[rep]
    slot_of = (leaving, 1 - leaving)
    copies = []
    offsets, lengths = [], []
    for n, slot in enumerate(slot_of):
        length = cache_len[rep * slots + slot]
        first = length + 1 - WIN
        start = pl.multiple_of(
            jnp.minimum(lax.div(first, ROW_TILE) * ROW_TILE, capacity - COPY), ROW_TILE
        )
        offsets.append(first - start)
        lengths.append(length)
        for kv, cache in enumerate((cache_k, cache_v)):
            copies.append((
                pltpu.make_async_copy(
                    cache.at[slot, pl.ds(start, COPY)], body.at[n, kv], sems.at[n, kv, 0]
                ),
                pltpu.make_async_copy(
                    cache.at[slot, pl.ds(0, ROW_TILE)], sink.at[n, kv], sems.at[n, kv, 1]
                ),
            ))
    for pair in copies:
        for copy in pair:
            copy.start()

    row = lax.broadcasted_iota(jnp.int32, (8, width), 0)
    lane = lax.broadcasted_iota(jnp.int32, (8, width), 1)
    own = row == lax.div(lane, HD)
    head_row = lax.broadcasted_iota(jnp.int32, (8, COPY), 0)
    column = lax.broadcasted_iota(jnp.int32, (8, COPY), 1)
    slopes = jnp.zeros((8, COPY), F32)
    for h in range(local_heads):
        slopes = jnp.where(head_row == h, head_slope(local_heads, h), slopes)

    for n, slot in enumerate(slot_of):
        def newest(ref, slot=slot):
            both = ref[...].astype(F32)
            return jnp.where(slot == 0, both[0:1], both[1:2])

        windows = []
        for kv, new in enumerate((new_k, new_v)):
            for copy in copies[2 * n + kv]:
                copy.wait()
            rolled = pltpu.roll(
                body[n, kv].astype(F32), lax.rem(COPY + SINK - offsets[n], COPY), 0
            )
            top = jnp.where(row < SINK, sink[n, kv].astype(F32)[:8], rolled[:8])
            tail = jnp.where(row == SPAN - 1 - WIN, newest(new), rolled[WIN : WIN + 8])
            window = jnp.concatenate([top, rolled[8:WIN], tail, rolled[WIN + 8 :]], axis=0).astype(BF16)
            if n == 0:
                window_out[0, kv] = window[:SPAN]
            windows.append(window)
        query = jnp.where(own, newest(new_q), 0.0).astype(BF16)
        scores = dot(query, windows[0], ((1,), (1,))) * SCALE
        distance = jnp.where(column < SINK, lengths[n] - column, SPAN - 1 - column).astype(F32)
        scores = jnp.where(column < SPAN, scores - slopes * distance, MASKED)
        terms = jnp.exp2(scores - jnp.max(scores, axis=1, keepdims=True))
        weights = (terms / jnp.sum(terms, axis=1, keepdims=True)).astype(BF16)
        mixed = dot(weights, windows[1], ((1,), (0,)))
        mixed = jnp.sum(jnp.where(own, mixed, 0.0), axis=0, keepdims=True)
        (leave_out, stay_out)[n][...] = mixed.astype(BF16)


def decode(moving, cache_len, new_q, new_k, new_v, cache_k, cache_v):
    slots, _, width = cache_k.shape
    smem = pl.BlockSpec(memory_space=pltpu.SMEM)
    vmem = pl.BlockSpec(memory_space=pltpu.VMEM)
    hbm = pl.BlockSpec(memory_space=pl.ANY)
    return pl.pallas_call(
        decode_kernel,
        name="decode",
        out_shape=(
            jax.ShapeDtypeStruct((1, 2, SPAN, width), BF16),
            jax.ShapeDtypeStruct((1, width), BF16),
            jax.ShapeDtypeStruct((1, width), BF16),
        ),
        in_specs=[smem, smem, vmem, vmem, vmem, hbm, hbm],
        out_specs=(vmem, vmem, vmem),
        scratch_shapes=[
            pltpu.VMEM((2, 2, COPY, width), BF16),
            pltpu.VMEM((2, 2, ROW_TILE, width), BF16),
            pltpu.SemaphoreType.DMA((2, 2, 2)),
        ],
    )(moving, cache_len, new_q, new_k, new_v, cache_k, cache_v)


def prompt_kernel(length_ref, q_ref, k_ref, v_ref, out_ref, *, block):
    rows, width = q_ref.shape
    length = length_ref[0]
    for b in range(rows // block):
        keys = (b + 1) * block
        query_at = lax.broadcasted_iota(jnp.int32, (block, keys), 0) + b * block
        key_at = lax.broadcasted_iota(jnp.int32, (block, keys), 1)
        allowed = (key_at <= query_at) & (key_at < length)
        distance = (query_at - key_at).astype(F32)
        for h in range(width // HD):
            cols = slice(h * HD, (h + 1) * HD)
            scores = dot(
                q_ref[b * block : keys, cols], k_ref[:keys, cols], ((1,), (1,))
            ) * SCALE
            scores = jnp.where(
                allowed, scores - head_slope(width // HD, h) * distance, MASKED
            )
            terms = jnp.exp2(scores - jnp.max(scores, axis=1, keepdims=True))
            weights = (terms / jnp.sum(terms, axis=1, keepdims=True)).astype(BF16)
            out_ref[b * block : keys, cols] = dot(
                weights, v_ref[:keys, cols], ((1,), (0,))
            ).astype(BF16)


def prompt(length, q, k, v):
    vmem = pl.BlockSpec(memory_space=pltpu.VMEM)
    return pl.pallas_call(
        functools.partial(prompt_kernel, block=256),
        name="prompt",
        out_shape=jax.ShapeDtypeStruct(q.shape, BF16),
        in_specs=[pl.BlockSpec(memory_space=pltpu.SMEM), vmem, vmem, vmem],
        out_specs=vmem,
    )(length, q, k, v)


def project_kernel(x_ref, w_ref, bias_ref, residual_ref, hidden_ref, stream_ref, stats_ref):
    source = pl.program_id(0)
    part = dot(x_ref[0], w_ref[...], ((1,), (0,)))

    @pl.when(source == 0)
    def _():
        stream_ref[...] = part

    @pl.when(source > 0)
    def _():
        stream_ref[...] += part

    @pl.when(source == pl.num_programs(0) - 1)
    def _():
        stream = stream_ref[...] + bias_ref[...] + residual_ref[...].astype(F32)
        stream_ref[...] = stream
        hidden_ref[...] = stream.astype(BF16)
        width = stream.shape[1]
        mean = jnp.sum(stream, axis=1, keepdims=True) * (1.0 / width)
        centered = stream - mean
        spread = jnp.sum(centered * centered, axis=1, keepdims=True)
        lane = lax.broadcasted_iota(jnp.int32, (stream.shape[0], HD), 1)
        table = jnp.where(lane == 0, mean, jnp.where(lane == 1, spread, 0.0))
        pick = lax.broadcasted_iota(jnp.int32, (8, HD), 0) == lax.broadcasted_iota(jnp.int32, (8, HD), 1)
        stats_ref[...] = dot(pick.astype(F32), table, ((1,), (1,)), HIGHEST)[:2]


def project(gathered, weight, bias, residual):
    sources, rows, width = gathered.shape
    whole = lambda s: (0, 0)
    return pl.pallas_call(
        project_kernel,
        name="project",
        grid=(sources,),
        out_shape=(
            jax.ShapeDtypeStruct((rows, width), BF16),
            jax.ShapeDtypeStruct((rows, width), F32),
            jax.ShapeDtypeStruct((2, rows), F32),
        ),
        in_specs=[
            pl.BlockSpec((1, rows, width), lambda s: (s, 0, 0)),
            pl.BlockSpec((width, width), lambda s: (s, 0)),
            pl.BlockSpec((1, width), whole),
            pl.BlockSpec((rows, width), whole),
        ],
        out_specs=(
            pl.BlockSpec((rows, width), whole),
            pl.BlockSpec((rows, width), whole),
            pl.BlockSpec((2, rows), whole),
        ),
    )(gathered, weight, bias, residual)


def norm_kernel(stats_ref, stream_ref, gain_ref, shift_ref, out_ref):
    parts = stats_ref.shape[0]
    rows, width = stream_ref.shape
    means = stats_ref[:, 0, :]
    mean = jnp.sum(means, axis=0, keepdims=True) * (1.0 / parts)
    apart = means - mean
    spread = jnp.sum(stats_ref[:, 1, :] + width * (apart * apart), axis=0, keepdims=True)
    scale = lax.rsqrt(spread * (1.0 / (parts * width)) + EPSILON)
    row = lax.broadcasted_iota(jnp.int32, (8, rows), 0)
    table = jnp.where(row == 0, mean, jnp.where(row == 1, scale, 0.0))
    at = lax.broadcasted_iota(jnp.int32, (8, width), 0)
    mean_all = dot(table, (at == 0).astype(F32), ((0,), (0,)), HIGHEST)
    scale_all = dot(table, (at == 1).astype(F32), ((0,), (0,)), HIGHEST)
    out_ref[...] = (
        (stream_ref[...] - mean_all) * scale_all * gain_ref[...] + shift_ref[...]
    ).astype(BF16)


def norm(stats, stream, gain, shift):
    vmem = pl.BlockSpec(memory_space=pltpu.VMEM)
    return pl.pallas_call(
        norm_kernel,
        name="norm",
        out_shape=jax.ShapeDtypeStruct(stream.shape, BF16),
        in_specs=[vmem] * 4,
        out_specs=vmem,
    )(stats, stream, gain, shift)


def to_partner(block):
    count = lax.axis_size("rep")
    return lax.ppermute(block, "rep", [(i, (i + count // 2) % count) for i in range(count)])


def to_all(block):
    count = lax.axis_size("tp")
    return lax.all_to_all(jnp.broadcast_to(block[None], (count, *block.shape)), "tp", 0, 0)


def on_device(
    prompt_q, prompt_k, prompt_v, prompt_len, cache_keys, cache_values, new_q, new_k, new_v,
    cache_len, moving, out_weight, out_bias, residual, ln_gain, ln_shift,
):
    window, stay_row, leave_row = decode(
        moving, cache_len, new_q, new_k, new_v, cache_keys, cache_values
    )
    come_row = to_partner(leave_row)
    moved_window = to_partner(window)
    prompt_mix = prompt(prompt_len, prompt_q, prompt_k, prompt_v)
    mixed_rows = jnp.concatenate([prompt_mix, stay_row, come_row], axis=0)
    hidden_out, stream, stats = project(
        to_all(mixed_rows), out_weight, out_bias[None], residual
    )
    normed = norm(to_all(stats), stream, ln_gain[None], ln_shift[None])
    return (hidden_out, normed, moved_window)


def solution(mesh):
    in_specs = (
        P("rep", "tp"), P("rep", "tp"), P("rep", "tp"), P("rep"),
        P("rep", None, "tp"), P("rep", None, "tp"),
        P("rep", "tp"), P("rep", "tp"), P("rep", "tp"),
        P(), P(), P(None, "tp"), P("tp"), P("rep", "tp"), P("tp"), P("tp"),
    )
    out_specs = (P("rep", "tp"), P("rep", "tp"), P("rep", None, None, "tp"))
    return jax.shard_map(
        on_device, mesh=mesh, in_specs=in_specs, out_specs=out_specs, check_vma=False
    )
```

```python
import functools
import math

import jax
import jax.numpy as jnp
from jax import lax
from jax.experimental import pallas as pl
from jax.experimental.pallas import tpu as pltpu
from jax.sharding import PartitionSpec as P

D = 2048
HEADS = 16
HD = 128
SINK = 4
WIN = 256
SPAN = SINK + WIN
ROW_TILE = 16
COPY = 272

LOG2E = math.log2(math.e)
SCALE = LOG2E / math.sqrt(HD)
MASKED = -1e30
EPSILON = 1e-05
BLOCK = 128
ROOM = 16 * 2**20

F32 = jnp.float32
BF16 = jnp.bfloat16
HIGHEST = lax.Precision.HIGHEST

SMEM = pl.BlockSpec(memory_space=pltpu.SMEM)
VMEM = pl.BlockSpec(memory_space=pltpu.VMEM)
HBM = pl.BlockSpec(memory_space=pl.ANY)


def kept(shape, dtype):
    return pltpu.VMEM(shape, dtype)


def placed(shape, dtype):
    return pltpu.HBM(shape, dtype)


def near(array):
    return pltpu.with_memory_space_constraint(array, pltpu.VMEM)


def far(array):
    return pltpu.with_memory_space_constraint(array, pltpu.HBM)


def dot(a, b, contract, precision=None):
    return lax.dot_general(a, b, (contract, ((), ())), precision=precision, preferred_element_type=F32)


def head_slope(local_heads, head):
    tp = lax.axis_index("tp")
    slope = jnp.float32(LOG2E * 2.0 ** (-8.0 * (head + 1) / HEADS))
    step = 2.0 ** (-8.0 * local_heads / HEADS)
    for k in range(1, HEADS // local_heads):
        slope = jnp.where(tp >= k, slope * step, slope)
    return slope


def decode_kernel(
    moving_hbm, cache_len_hbm, new_q_hbm, new_k_hbm, new_v_hbm, cache_k, cache_v,
    window_out, stay_out, leave_out, moving, cache_len, new_q, new_k, new_v, body, sink, sems, small_sems,
):
    small = [
        pltpu.make_async_copy(source, target, small_sems.at[i])
        for i, (source, target) in enumerate((
            (moving_hbm, moving), (cache_len_hbm, cache_len),
            (new_q_hbm, new_q), (new_k_hbm, new_k), (new_v_hbm, new_v),
        ))
    ]
    for copy in small:
        copy.start()
    small[0].wait()
    small[1].wait()
    rep = lax.axis_index("rep")
    slots, capacity, width = cache_k.shape
    local_heads = width // HD
    leaving = moving[rep]
    slot_of = (leaving, 1 - leaving)
    copies = []
    offsets, lengths = [], []
    for n, slot in enumerate(slot_of):
        length = cache_len[rep * slots + slot]
        first = length + 1 - WIN
        start = pl.multiple_of(
            jnp.minimum(lax.div(first, ROW_TILE) * ROW_TILE, capacity - COPY), ROW_TILE
        )
        offsets.append(first - start)
        lengths.append(length)
        for kv, cache in enumerate((cache_k, cache_v)):
            copies.append((
                pltpu.make_async_copy(
                    cache.at[slot, pl.ds(start, COPY)], body.at[n, kv], sems.at[n, kv, 0]
                ),
                pltpu.make_async_copy(
                    cache.at[slot, pl.ds(0, ROW_TILE)], sink.at[n, kv], sems.at[n, kv, 1]
                ),
            ))
    for pair in copies:
        for copy in pair:
            copy.start()

    for copy in small[2:]:
        copy.wait()

    row = lax.broadcasted_iota(jnp.int32, (8, width), 0)
    lane = lax.broadcasted_iota(jnp.int32, (8, width), 1)
    own = row == lax.div(lane, HD)
    head_row = lax.broadcasted_iota(jnp.int32, (8, COPY), 0)
    column = lax.broadcasted_iota(jnp.int32, (8, COPY), 1)
    slopes = jnp.zeros((8, COPY), F32)
    for h in range(local_heads):
        slopes = jnp.where(head_row == h, head_slope(local_heads, h), slopes)

    for n, slot in enumerate(slot_of):
        def newest(ref, slot=slot):
            both = ref[...].astype(F32)
            return jnp.where(slot == 0, both[0:1], both[1:2])

        windows = []
        for kv, new in enumerate((new_k, new_v)):
            for copy in copies[2 * n + kv]:
                copy.wait()
            rolled = pltpu.roll(
                body[n, kv].astype(F32), lax.rem(COPY + SINK - offsets[n], COPY), 0
            )
            top = jnp.where(row < SINK, sink[n, kv].astype(F32)[:8], rolled[:8])
            tail = jnp.where(row == SPAN - 1 - WIN, newest(new), rolled[WIN : WIN + 8])
            window = jnp.concatenate([top, rolled[8:WIN], tail, rolled[WIN + 8 :]], axis=0).astype(BF16)
            if n == 0:
                window_out[0, kv] = window[:SPAN]
            windows.append(window)
        query = jnp.where(own, newest(new_q), 0.0).astype(BF16)
        scores = dot(query, windows[0], ((1,), (1,))) * SCALE
        distance = jnp.where(column < SINK, lengths[n] - column, SPAN - 1 - column).astype(F32)
        scores = jnp.where(column < SPAN, scores - slopes * distance, MASKED)
        terms = jnp.exp2(scores - jnp.max(scores, axis=1, keepdims=True))
        weights = (terms / jnp.sum(terms, axis=1, keepdims=True)).astype(BF16)
        mixed = dot(weights, windows[1], ((1,), (0,)))
        mixed = jnp.sum(jnp.where(own, mixed, 0.0), axis=0, keepdims=True)
        (leave_out, stay_out)[n][...] = mixed.astype(BF16)


def decode(moving, cache_len, new_q, new_k, new_v, cache_k, cache_v):
    width = cache_k.shape[2]
    return pl.pallas_call(
        decode_kernel,
        name="decode",
        compiler_params=pltpu.CompilerParams(vmem_limit_bytes=ROOM),
        out_shape=(
            jax.ShapeDtypeStruct((1, 2, SPAN, width), BF16),
            jax.ShapeDtypeStruct((1, width), BF16),
            jax.ShapeDtypeStruct((1, width), BF16),
        ),
        in_specs=[HBM] * 7,
        out_specs=(VMEM, VMEM, VMEM),
        scratch_shapes=[
            pltpu.SMEM(moving.shape, jnp.int32),
            pltpu.SMEM(cache_len.shape, jnp.int32),
            *[pltpu.VMEM(new_q.shape, BF16)] * 3,
            pltpu.VMEM((2, 2, COPY, width), BF16),
            pltpu.VMEM((2, 2, ROW_TILE, width), BF16),
            pltpu.SemaphoreType.DMA((2, 2, 2)),
            pltpu.SemaphoreType.DMA((5,)),
        ],
    )(*map(far, (moving, cache_len, new_q, new_k, new_v, cache_k, cache_v)))


def prompt_kernel(
    length_ref, q_ref, k_ref, v_ref, stay_ref, come_ref, out_hbm, out_ref, sems, *, block,
):
    rows, width = q_ref.shape
    row = lax.broadcasted_iota(jnp.int32, (8, width), 0)
    served = jnp.where(row == 0, stay_ref[...].astype(F32), jnp.where(row == 1, come_ref[...].astype(F32), 0.0))
    out_ref[rows:] = served.astype(BF16)
    length = length_ref[0]
    copies = []
    for step, first in enumerate(range(0, rows, block)):
        keys = first + block
        query_at = lax.broadcasted_iota(jnp.int32, (block, keys), 0) + first
        key_at = lax.broadcasted_iota(jnp.int32, (block, keys), 1)
        allowed = (key_at <= query_at) & (key_at < length)
        distance = (query_at - key_at).astype(F32)
        for h in range(width // HD):
            cols = slice(h * HD, (h + 1) * HD)
            scores = dot(q_ref[first:keys, cols], k_ref[:keys, cols], ((1,), (1,))) * SCALE
            scores = jnp.where(allowed, scores - head_slope(width // HD, h) * distance, MASKED)
            terms = jnp.exp2(scores - jnp.max(scores, axis=1, keepdims=True))
            weights = (terms / jnp.sum(terms, axis=1, keepdims=True)).astype(BF16)
            out_ref[first:keys, cols] = dot(weights, v_ref[:keys, cols], ((1,), (0,))).astype(BF16)
        done = slice(first, keys if keys < rows else rows + 8)
        for member in range(out_hbm.shape[0]):
            copy = pltpu.make_async_copy(out_ref.at[done], out_hbm.at[member, done], sems.at[step, member])
            copy.start()
            copies.append(copy)
    for copy in copies:
        copy.wait()


def prompt(length, q, k, v, stay_row, come_row, members):
    rows, width = q.shape
    block = 256
    return pl.pallas_call(
        functools.partial(prompt_kernel, block=block),
        name="prompt",
        compiler_params=pltpu.CompilerParams(vmem_limit_bytes=ROOM),
        out_shape=placed((members, rows + 8, width), BF16),
        in_specs=[SMEM, VMEM, VMEM, VMEM, VMEM, VMEM],
        out_specs=HBM,
        scratch_shapes=[
            pltpu.VMEM((rows + 8, width), BF16),
            pltpu.SemaphoreType.DMA((rows // block, members)),
        ],
    )(length, near(q), near(k), near(v), stay_row, come_row)


def project_kernel(x_ref, w_ref, bias_ref, residual_hbm, hidden_ref, stream_hbm, stats_ref, residual_ref, sum_ref, sem):
    copy = pltpu.make_async_copy(residual_hbm, residual_ref, sem)
    copy.start()
    sources, _, width = x_ref.shape
    rows = sum_ref.shape[0]
    blocks = [slice(start, min(start + BLOCK, rows)) for start in range(0, rows, BLOCK)]
    for at in blocks:
        sum_ref[at] = sum(
            dot(x_ref[s, at], w_ref[s * width : (s + 1) * width], ((1,), (0,))) for s in range(sources)
        )
    copy.wait()
    for at in blocks:
        size = at.stop - at.start
        stream = sum_ref[at] + bias_ref[...] + residual_ref[at].astype(F32)
        sum_ref[at] = stream
        hidden_ref[at] = stream.astype(BF16)
        mean = jnp.sum(stream, axis=1, keepdims=True) * (1.0 / width)
        centered = stream - mean
        spread = jnp.sum(centered * centered, axis=1, keepdims=True)
        lane = lax.broadcasted_iota(jnp.int32, (size, HD), 1)
        table = jnp.where(lane == 0, mean, jnp.where(lane == 1, spread, 0.0))
        stats = table.T[:2]
        for copy in range(stats_ref.shape[0]):
            stats_ref[copy, :, at] = stats
    out = pltpu.make_async_copy(sum_ref, stream_hbm, sem)
    out.start()
    out.wait()


def project(gathered, weight, bias, residual):
    sources = gathered.shape[0]
    rows, width = residual.shape
    return pl.pallas_call(
        project_kernel,
        name="project",
        compiler_params=pltpu.CompilerParams(vmem_limit_bytes=ROOM),
        out_shape=(
            kept((rows, width), BF16),
            placed((rows, width), F32),
            placed((sources, 2, rows), F32),
        ),
        in_specs=[VMEM, VMEM, VMEM, HBM],
        out_specs=(VMEM, HBM, VMEM),
        scratch_shapes=[
            pltpu.VMEM((rows, width), BF16),
            pltpu.VMEM((rows, width), F32),
            pltpu.SemaphoreType.DMA,
        ],
    )(near(gathered), near(weight), bias, far(residual))


def norm_kernel(stats_ref, stream_hbm, gain_ref, shift_ref, out_ref, stream_ref, sem):
    copy = pltpu.make_async_copy(stream_hbm, stream_ref, sem)
    copy.start()
    parts = stats_ref.shape[0]
    rows, width = stream_ref.shape
    means = stats_ref[:, 0, :]
    mean = jnp.sum(means, axis=0, keepdims=True) * (1.0 / parts)
    apart = means - mean
    spread = jnp.sum(stats_ref[:, 1, :] + width * (apart * apart), axis=0, keepdims=True)
    scale = lax.rsqrt(spread * (1.0 / (parts * width)) + EPSILON)
    row = lax.broadcasted_iota(jnp.int32, (8, rows), 0)
    table = jnp.where(row == 0, mean, jnp.where(row == 1, scale, 0.0))
    copy.wait()
    for start in range(0, rows, BLOCK):
        at = slice(start, min(start + BLOCK, rows))
        columns = table[:, at].T
        out_ref[at] = (
            (stream_ref[at] - columns[:, 0:1]) * columns[:, 1:2] * gain_ref[...] + shift_ref[...]
        ).astype(BF16)


def norm(stats, stream, gain, shift):
    return pl.pallas_call(
        norm_kernel,
        name="norm",
        compiler_params=pltpu.CompilerParams(vmem_limit_bytes=ROOM),
        out_shape=jax.ShapeDtypeStruct(stream.shape, BF16),
        in_specs=[VMEM, HBM, VMEM, VMEM],
        out_specs=VMEM,
        scratch_shapes=[pltpu.VMEM(stream.shape, F32), pltpu.SemaphoreType.DMA],
    )(near(stats), far(stream), gain, shift)


def to_partner(block):
    count = lax.axis_size("rep")
    return lax.ppermute(block, "rep", [(i, (i + count // 2) % count) for i in range(count)])


def exchange(blocks):
    return lax.all_to_all(blocks, "tp", 0, 0)


def after(values, other):
    return lax.optimization_barrier((values, other))[0]


def on_device(
    prompt_q, prompt_k, prompt_v, prompt_len, cache_keys, cache_values, new_q, new_k, new_v,
    cache_len, moving, out_weight, out_bias, residual, ln_gain, ln_shift,
):
    window, stay_row, leave_row = decode(
        moving, cache_len, new_q, new_k, new_v, cache_keys, cache_values
    )
    come_row = to_partner(leave_row)
    window, leave_row = lax.optimization_barrier((window, leave_row))
    moved_window = to_partner(window)
    mixed = prompt(
        prompt_len, prompt_q, prompt_k, prompt_v, stay_row, come_row, lax.axis_size("tp")
    )
    hidden_out, stream, stats = project(exchange(mixed), out_weight, out_bias[None], residual)
    normed = norm(exchange(stats), stream, ln_gain[None], ln_shift[None])
    return (hidden_out, normed, moved_window)


def solution(mesh):
    in_specs = (
        P("rep", "tp"), P("rep", "tp"), P("rep", "tp"), P("rep"),
        P("rep", None, "tp"), P("rep", None, "tp"),
        P("rep", "tp"), P("rep", "tp"), P("rep", "tp"),
        P(), P(), P(None, "tp"), P("tp"), P("rep", "tp"), P("tp"), P("tp"),
    )
    out_specs = (P("rep", "tp"), P("rep", "tp"), P("rep", None, None, "tp"))
    return jax.shard_map(
        on_device, mesh=mesh, in_specs=in_specs, out_specs=out_specs, check_vma=False
    )
```

```python
import functools
import math

import jax
import jax.numpy as jnp
from jax import lax
from jax.experimental import pallas as pl
from jax.experimental.pallas import tpu as pltpu
from jax.sharding import PartitionSpec as P

D = 2048
HEADS = 16
HD = 128
SINK = 4
WIN = 256
SPAN = SINK + WIN
ROW_TILE = 16
COPY = 272

LOG2E = math.log2(math.e)
SCALE = LOG2E / math.sqrt(HD)
MASKED = -1e30
EPSILON = 1e-05
BLOCK = 128
ROOM = 16 * 2**20

F32 = jnp.float32
BF16 = jnp.bfloat16
HIGHEST = lax.Precision.HIGHEST

SMEM = pl.BlockSpec(memory_space=pltpu.SMEM)
VMEM = pl.BlockSpec(memory_space=pltpu.VMEM)
HBM = pl.BlockSpec(memory_space=pl.ANY)


def kept(shape, dtype):
    return pltpu.VMEM(shape, dtype)


def placed(shape, dtype):
    return pltpu.HBM(shape, dtype)


def near(array):
    return pltpu.with_memory_space_constraint(array, pltpu.VMEM)


def far(array):
    return pltpu.with_memory_space_constraint(array, pltpu.HBM)


def dot(a, b, contract, precision=None):
    return lax.dot_general(a, b, (contract, ((), ())), precision=precision, preferred_element_type=F32)


def core_of():
    return lax.rem(lax.axis_index("rep"), 2)


def side_of():
    return lax.rem(lax.div(lax.axis_index("tp"), 2), 2)


def head_slope(local_heads, head):
    tp = lax.axis_index("tp")
    slope = jnp.float32(LOG2E * 2.0 ** (-8.0 * (head + 1) / HEADS))
    step = 2.0 ** (-8.0 * local_heads / HEADS)
    for k in range(1, HEADS // local_heads):
        slope = jnp.where(tp >= k, slope * step, slope)
    return slope


def decode_kernel(
    moving_hbm, cache_len_hbm, new_q_hbm, new_k_hbm, new_v_hbm, cache_k, cache_v, weight_hbm, residual_hbm, bias_hbm,
    window_out, stay_out, leave_out, packed_ref,
    moving, cache_len, new_q, new_k, new_v, body, sink, sems, small_sems, residual_ref, bias_ref, pack_sems,
):
    part = weight_hbm.shape[0] // 2
    weight_copy = pltpu.make_async_copy(
        weight_hbm.at[pl.ds(pl.multiple_of(core_of() * part, part), part)],
        packed_ref.at[pl.ds(0, part)],
        pack_sems.at[0],
    )
    residual_copy = pltpu.make_async_copy(residual_hbm, residual_ref, pack_sems.at[1])
    bias_copy = pltpu.make_async_copy(bias_hbm, bias_ref, pack_sems.at[2])
    small = [
        pltpu.make_async_copy(source, target, small_sems.at[i])
        for i, (source, target) in enumerate((
            (moving_hbm, moving), (cache_len_hbm, cache_len),
            (new_q_hbm, new_q), (new_k_hbm, new_k), (new_v_hbm, new_v),
        ))
    ]
    for copy in small:
        copy.start()
    small[0].wait()
    small[1].wait()
    rep = lax.axis_index("rep")
    slots, capacity, width = cache_k.shape
    local_heads = width // HD
    leaving = moving[rep]
    slot_of = (leaving, 1 - leaving)
    copies = []
    offsets, lengths = [], []
    for n, slot in enumerate(slot_of):
        length = cache_len[rep * slots + slot]
        first = length + 1 - WIN
        start = pl.multiple_of(
            jnp.minimum(lax.div(first, ROW_TILE) * ROW_TILE, capacity - COPY), ROW_TILE
        )
        offsets.append(first - start)
        lengths.append(length)
        for kv, cache in enumerate((cache_k, cache_v)):
            copies.append((
                pltpu.make_async_copy(
                    cache.at[slot, pl.ds(start, COPY)], body.at[n, kv], sems.at[n, kv, 0]
                ),
                pltpu.make_async_copy(
                    cache.at[slot, pl.ds(0, ROW_TILE)], sink.at[n, kv], sems.at[n, kv, 1]
                ),
            ))
    for pair in copies:
        for copy in pair:
            copy.start()
    residual_copy.start()
    bias_copy.start()
    weight_copy.start()

    for copy in small[2:]:
        copy.wait()

    row = lax.broadcasted_iota(jnp.int32, (8, width), 0)
    lane = lax.broadcasted_iota(jnp.int32, (8, width), 1)
    own = row == lax.div(lane, HD)
    head_row = lax.broadcasted_iota(jnp.int32, (8, COPY), 0)
    column = lax.broadcasted_iota(jnp.int32, (8, COPY), 1)
    slopes = jnp.zeros((8, COPY), F32)
    for h in range(local_heads):
        slopes = jnp.where(head_row == h, head_slope(local_heads, h), slopes)

    for n, slot in enumerate(slot_of):
        def newest(ref, slot=slot):
            both = ref[...].astype(F32)
            return jnp.where(slot == 0, both[0:1], both[1:2])

        windows = []
        for kv, new in enumerate((new_k, new_v)):
            for copy in copies[2 * n + kv]:
                copy.wait()
            rolled = pltpu.roll(
                body[n, kv].astype(F32), lax.rem(COPY + SINK - offsets[n], COPY), 0
            )
            top = jnp.where(row < SINK, sink[n, kv].astype(F32)[:8], rolled[:8])
            tail = jnp.where(row == SPAN - 1 - WIN, newest(new), rolled[WIN : WIN + 8])
            window = jnp.concatenate([top, rolled[8:WIN], tail, rolled[WIN + 8 :]], axis=0).astype(BF16)
            if n == 0:
                window_out[0, kv] = window[:SPAN]
            windows.append(window)
        query = jnp.where(own, newest(new_q), 0.0).astype(BF16)
        scores = dot(query, windows[0], ((1,), (1,))) * SCALE
        distance = jnp.where(column < SINK, lengths[n] - column, SPAN - 1 - column).astype(F32)
        scores = jnp.where(column < SPAN, scores - slopes * distance, MASKED)
        terms = jnp.exp2(scores - jnp.max(scores, axis=1, keepdims=True))
        weights = (terms / jnp.sum(terms, axis=1, keepdims=True)).astype(BF16)
        mixed = dot(weights, windows[1], ((1,), (0,)))
        mixed = jnp.sum(jnp.where(own, mixed, 0.0), axis=0, keepdims=True)
        (leave_out, stay_out)[n][...] = mixed.astype(BF16)

    residual_copy.wait()
    bias_copy.wait()
    half = (residual_ref.shape[0] - 2) // 2
    lower, upper = residual_ref[: half + 8].astype(F32), residual_ref[half:].astype(F32)
    upper = jnp.concatenate([upper, jnp.zeros((6, width), F32)], axis=0)
    packed_ref[part : part + half + 8] = jnp.where(side_of() == 0, upper, lower).astype(BF16)
    bias = bias_ref[...]
    high = bias.astype(BF16).astype(F32)
    packed_ref[part + half + 8 :] = jnp.where(row == 0, high, jnp.where(row == 1, bias - high, 0.0)).astype(BF16)
    weight_copy.wait()


def decode(moving, cache_len, new_q, new_k, new_v, cache_k, cache_v, weight, residual, bias):
    width = cache_k.shape[2]
    tail = (residual.shape[0] - 2) // 2 + 16
    return pl.pallas_call(
        decode_kernel,
        name="decode",
        compiler_params=pltpu.CompilerParams(vmem_limit_bytes=ROOM),
        out_shape=(
            jax.ShapeDtypeStruct((1, 2, SPAN, width), BF16),
            jax.ShapeDtypeStruct((1, width), BF16),
            jax.ShapeDtypeStruct((1, width), BF16),
            kept((weight.shape[0] // 2 + tail, width), BF16),
        ),
        in_specs=[HBM] * 10,
        out_specs=(VMEM,) * 4,
        scratch_shapes=[
            pltpu.SMEM(moving.shape, jnp.int32),
            pltpu.SMEM(cache_len.shape, jnp.int32),
            *[pltpu.VMEM(new_q.shape, BF16)] * 3,
            pltpu.VMEM((2, 2, COPY, width), BF16),
            pltpu.VMEM((2, 2, ROW_TILE, width), BF16),
            pltpu.SemaphoreType.DMA((2, 2, 2)),
            pltpu.SemaphoreType.DMA((5,)),
            pltpu.VMEM(residual.shape, BF16),
            pltpu.VMEM((1, width), F32),
            pltpu.SemaphoreType.DMA((3,)),
        ],
    )(*map(far, (moving, cache_len, new_q, new_k, new_v, cache_k, cache_v, weight, residual, bias)))


def prompt_kernel(
    length_ref, q_ref, k_ref, v_ref, stay_ref, come_ref, out_hbm, out_ref, sems, *, block,
):
    rows, width = q_ref.shape
    row = lax.broadcasted_iota(jnp.int32, (8, width), 0)
    served = jnp.where(row == 0, stay_ref[...].astype(F32), jnp.where(row == 1, come_ref[...].astype(F32), 0.0))
    out_ref[rows:] = served.astype(BF16)
    length = length_ref[0]
    copies = []
    for step, first in enumerate(range(0, rows, block)):
        keys = first + block
        query_at = lax.broadcasted_iota(jnp.int32, (block, keys), 0) + first
        key_at = lax.broadcasted_iota(jnp.int32, (block, keys), 1)
        allowed = (key_at <= query_at) & (key_at < length)
        distance = (query_at - key_at).astype(F32)
        for h in range(width // HD):
            cols = slice(h * HD, (h + 1) * HD)
            scores = dot(q_ref[first:keys, cols], k_ref[:keys, cols], ((1,), (1,))) * SCALE
            scores = jnp.where(allowed, scores - head_slope(width // HD, h) * distance, MASKED)
            terms = jnp.exp2(scores - jnp.max(scores, axis=1, keepdims=True))
            weights = (terms / jnp.sum(terms, axis=1, keepdims=True)).astype(BF16)
            out_ref[first:keys, cols] = dot(weights, v_ref[:keys, cols], ((1,), (0,))).astype(BF16)
        for member in range(out_hbm.shape[0]):
            lower = member // 2 % 2 == 0
            if lower and step == 0:
                here, there = slice(0, block), slice(0, block)
            elif lower:
                here, there = slice(block, block + 8), slice(block, block + 8)
            elif step == 1:
                here, there = slice(block, rows + 8), slice(0, block + 8)
            else:
                continue
            copy = pltpu.make_async_copy(out_ref.at[here], out_hbm.at[member, there], sems.at[step, member])
            copy.start()
            copies.append(copy)
    for copy in copies:
        copy.wait()


def prompt(length, q, k, v, stay_row, come_row, members):
    rows, width = q.shape
    block = rows // 2
    return pl.pallas_call(
        functools.partial(prompt_kernel, block=block),
        name="prompt",
        compiler_params=pltpu.CompilerParams(vmem_limit_bytes=ROOM),
        out_shape=placed((members, block + 8, width), BF16),
        in_specs=[SMEM, VMEM, VMEM, VMEM, VMEM, VMEM],
        out_specs=HBM,
        scratch_shapes=[
            pltpu.VMEM((rows + 8, width), BF16),
            pltpu.SemaphoreType.DMA((rows // block, members)),
        ],
    )(length, near(q), near(k), near(v), stay_row, come_row)


def project_kernel(
    x_ref, w_ref, packed_ref, swapped_ref, bias_ref, residual_hbm,
    own_hbm, pair_hbm, stats_ref, residual_ref, own_ref, pair_ref, sems,
):
    residual_copy = pltpu.make_async_copy(residual_hbm, residual_ref, sems.at[0])
    residual_copy.start()
    sources, rows, width = x_ref.shape
    part = sources // 2
    core, side = core_of(), side_of()
    near_half, far_half = core * part, (1 - core) * part
    blocks = [slice(start, min(start + BLOCK, rows)) for start in range(0, rows, BLOCK)]
    for at in blocks:
        pair_ref[at] = sum(
            dot(x_ref[near_half + s, at], packed_ref[s * width : (s + 1) * width], ((1,), (0,)))
            + dot(x_ref[far_half + s, at], swapped_ref[s * width : (s + 1) * width], ((1,), (0,)))
            for s in range(part)
        )
        own_ref[at] = sum(
            dot(x_ref[s, at], w_ref[s * width : (s + 1) * width], ((1,), (0,))) for s in range(sources)
        )
    residual_copy.wait()
    extra = part * width
    pair_bias = packed_ref[extra + rows :].astype(F32)
    pair_bias = pair_bias[0:1] + pair_bias[1:2]
    copies = []
    for step, at in enumerate(blocks):
        size = at.stop - at.start
        upper = residual_ref[at.start + rows - 8 : min(at.stop + rows - 8, residual_ref.shape[0])].astype(F32)
        if upper.shape[0] < size:
            upper = jnp.concatenate([upper, jnp.zeros((size - upper.shape[0], width), F32)], axis=0)
        own = own_ref[at] + bias_ref[...] + jnp.where(side == 0, residual_ref[at].astype(F32), upper)
        pair = pair_ref[at] + pair_bias + packed_ref[extra + at.start : extra + at.stop].astype(F32)
        own_ref[at] = own
        pair_ref[at] = pair
        for k, (source, target) in enumerate(((own_ref, own_hbm), (pair_ref, pair_hbm))):
            copy = pltpu.make_async_copy(source.at[at], target.at[at], sems.at[1 + 2 * step + k])
            copy.start()
            copies.append(copy)
        mean = jnp.sum(own + pair, axis=1, keepdims=True) * (0.5 / width)
        own_centered, pair_centered = own - mean, pair - mean
        spread = jnp.sum(
            own_centered * own_centered + pair_centered * pair_centered, axis=1, keepdims=True
        )
        lane = lax.broadcasted_iota(jnp.int32, (size, HD), 1)
        table = jnp.where(lane == 0, mean, jnp.where(lane == 1, spread, 0.0))
        stats = table.T[:2]
        for member in range(stats_ref.shape[0]):
            stats_ref[member, :, at] = stats
    for copy in copies:
        copy.wait()


def project(gathered, weight, packed, swapped, bias, residual):
    sources, rows, width = gathered.shape
    steps = -(-rows // BLOCK)
    return pl.pallas_call(
        project_kernel,
        name="project",
        compiler_params=pltpu.CompilerParams(vmem_limit_bytes=ROOM),
        out_shape=(
            placed((rows, width), F32),
            placed((rows, width), F32),
            placed((sources, 2, rows), F32),
        ),
        in_specs=[VMEM] * 5 + [HBM],
        out_specs=(HBM, HBM, VMEM),
        scratch_shapes=[
            pltpu.VMEM(residual.shape, BF16),
            pltpu.VMEM((rows, width), F32),
            pltpu.VMEM((rows, width), F32),
            pltpu.SemaphoreType.DMA((1 + 2 * steps,)),
        ],
    )(near(gathered), near(weight), near(packed), near(swapped), bias, far(residual))


def norm_kernel(
    stats_ref, own_hbm, come_hbm, gain_ref, shift_ref, hidden_ref, normed_ref, own_ref, come_ref, sems,
):
    copies = [
        pltpu.make_async_copy(source, target, sems.at[i])
        for i, (source, target) in enumerate(((own_hbm, own_ref), (come_hbm, come_ref)))
    ]
    for copy in copies:
        copy.start()
    members = stats_ref.shape[0]
    rows, width = own_ref.shape
    parts = members // 2
    side = side_of()
    tables = []
    for half in range(2):
        sources = [s for s in range(members) if s // 2 % 2 == half]
        means = [stats_ref[s, 0:1, :] for s in sources]
        mean = sum(means) * (1.0 / parts)
        spread = sum(
            stats_ref[s, 1:2, :] + (2 * width) * ((part - mean) * (part - mean))
            for s, part in zip(sources, means)
        )
        scale = lax.rsqrt(spread * (1.0 / (members * width)) + EPSILON)
        row = lax.broadcasted_iota(jnp.int32, (8, rows), 0)
        tables.append(jnp.where(row == 0, mean, jnp.where(row == 1, scale, 0.0)))
    for copy in copies:
        copy.wait()
    total = hidden_ref.shape[0]
    for half, table in enumerate(tables):
        first = half * (rows - 8)
        used = rows - 8 if half == 0 else total - first
        for start in range(0, used, BLOCK):
            at = slice(start, min(start + BLOCK, used))
            columns = table[:, at].T
            own, come = own_ref[at], come_ref[at]
            stream = jnp.where(side == half, own, come)
            to = slice(first + at.start, first + at.stop)
            hidden_ref[to] = stream.astype(BF16)
            normed_ref[to] = (
                (stream - columns[:, 0:1]) * columns[:, 1:2] * gain_ref[...] + shift_ref[...]
            ).astype(BF16)


def norm(stats, own, come, gain, shift, rows):
    out = jax.ShapeDtypeStruct((rows, own.shape[1]), BF16)
    return pl.pallas_call(
        norm_kernel,
        name="norm",
        compiler_params=pltpu.CompilerParams(vmem_limit_bytes=ROOM),
        out_shape=(out, out),
        in_specs=[VMEM, HBM, HBM, VMEM, VMEM],
        out_specs=(VMEM, VMEM),
        scratch_shapes=[
            pltpu.VMEM(own.shape, F32),
            pltpu.VMEM(own.shape, F32),
            pltpu.SemaphoreType.DMA((2,)),
        ],
    )(near(stats), far(own), far(come), gain, shift)


def to_partner(block):
    count = lax.axis_size("rep")
    return lax.ppermute(block, "rep", [(i, (i + count // 2) % count) for i in range(count)])


def to_pair(block):
    return lax.ppermute(block, "tp", [(i, i ^ 2) for i in range(lax.axis_size("tp"))])


def to_sibling(block):
    return lax.ppermute(block, "rep", [(i, i ^ 1) for i in range(lax.axis_size("rep"))])


def exchange(blocks):
    return lax.all_to_all(blocks, "tp", 0, 0)


def after(values, other):
    return lax.optimization_barrier((values, other))[0]


def on_device(
    prompt_q, prompt_k, prompt_v, prompt_len, cache_keys, cache_values, new_q, new_k, new_v,
    cache_len, moving, out_weight, out_bias, residual, ln_gain, ln_shift,
):
    window, stay_row, leave_row, packed = decode(
        moving, cache_len, new_q, new_k, new_v, cache_keys, cache_values, out_weight, residual, out_bias[None]
    )
    come_row = to_partner(leave_row)
    packed = to_pair(packed)
    swapped = to_sibling(packed)
    moved_window = to_partner(window)
    mixed = prompt(
        prompt_len, prompt_q, prompt_k, prompt_v, stay_row, come_row, lax.axis_size("tp")
    )
    own, pair, stats = project(
        exchange(mixed), out_weight, packed, swapped, out_bias[None], residual
    )
    stats = exchange(stats)
    hidden_out, normed = norm(
        stats, own, to_pair(pair), ln_gain[None], ln_shift[None], residual.shape[0]
    )
    return (hidden_out, normed, moved_window)


def solution(mesh):
    in_specs = (
        P("rep", "tp"), P("rep", "tp"), P("rep", "tp"), P("rep"),
        P("rep", None, "tp"), P("rep", None, "tp"),
        P("rep", "tp"), P("rep", "tp"), P("rep", "tp"),
        P(), P(), P(None, "tp"), P("tp"), P("rep", "tp"), P("tp"), P("tp"),
    )
    out_specs = (P("rep", "tp"), P("rep", "tp"), P("rep", None, None, "tp"))
    return jax.shard_map(
        on_device, mesh=mesh, in_specs=in_specs, out_specs=out_specs, check_vma=False
    )
```

```python
import functools
import math

import jax
import jax.numpy as jnp
from jax import lax
from jax.experimental import pallas as pl
from jax.experimental.pallas import tpu as pltpu
from jax.sharding import PartitionSpec as P

D = 2048
HEADS = 16
HD = 128
SINK = 4
WIN = 256
SPAN = SINK + WIN
ROW_TILE = 16
COPY = 272

LOG2E = math.log2(math.e)
SCALE = LOG2E / math.sqrt(HD)
MASKED = -1e30
EPSILON = 1e-05
BLOCK = 128
ROOM = 16 * 2**20

F32 = jnp.float32
BF16 = jnp.bfloat16
HIGHEST = lax.Precision.HIGHEST

SMEM = pl.BlockSpec(memory_space=pltpu.SMEM)
VMEM = pl.BlockSpec(memory_space=pltpu.VMEM)
HBM = pl.BlockSpec(memory_space=pl.ANY)


def kept(shape, dtype):
    return pltpu.VMEM(shape, dtype)


def placed(shape, dtype):
    return pltpu.HBM(shape, dtype)


def near(array):
    return pltpu.with_memory_space_constraint(array, pltpu.VMEM)


def far(array):
    return pltpu.with_memory_space_constraint(array, pltpu.HBM)


def dot(a, b, contract, precision=None):
    return lax.dot_general(a, b, (contract, ((), ())), precision=precision, preferred_element_type=F32)


def core_of():
    return lax.rem(lax.axis_index("rep"), 2)


def side_of():
    return lax.rem(lax.div(lax.axis_index("tp"), 2), 2)


def head_slope(local_heads, head):
    tp = lax.axis_index("tp")
    slope = jnp.float32(LOG2E * 2.0 ** (-8.0 * (head + 1) / HEADS))
    step = 2.0 ** (-8.0 * local_heads / HEADS)
    for k in range(1, HEADS // local_heads):
        slope = jnp.where(tp >= k, slope * step, slope)
    return slope


def decode_kernel(
    moving_hbm, cache_len_hbm, new_q_hbm, new_k_hbm, new_v_hbm, cache_k, cache_v, weight_hbm, residual_hbm, bias_hbm,
    window_out, stay_out, packed_ref,
    moving, cache_len, new_q, new_k, new_v, body, sink, sems, small_sems, residual_ref, bias_ref, pack_sems,
):
    part = weight_hbm.shape[0] // 2
    weight_copy = pltpu.make_async_copy(
        weight_hbm.at[pl.ds(pl.multiple_of(core_of() * part, part), part)],
        packed_ref.at[pl.ds(0, part)],
        pack_sems.at[0],
    )
    residual_copy = pltpu.make_async_copy(residual_hbm, residual_ref, pack_sems.at[1])
    bias_copy = pltpu.make_async_copy(bias_hbm, bias_ref, pack_sems.at[2])
    small = [
        pltpu.make_async_copy(source, target, small_sems.at[i])
        for i, (source, target) in enumerate((
            (moving_hbm, moving), (cache_len_hbm, cache_len),
            (new_q_hbm, new_q), (new_k_hbm, new_k), (new_v_hbm, new_v),
        ))
    ]
    for copy in small:
        copy.start()
    small[0].wait()
    small[1].wait()
    rep = lax.axis_index("rep")
    slots, capacity, width = cache_k.shape
    local_heads = width // HD
    leaving = moving[rep]
    slot_of = (leaving, 1 - leaving)
    copies = []
    offsets, lengths = [], []
    for n, slot in enumerate(slot_of):
        length = cache_len[rep * slots + slot]
        first = length + 1 - WIN
        start = pl.multiple_of(
            jnp.minimum(lax.div(first, ROW_TILE) * ROW_TILE, capacity - COPY), ROW_TILE
        )
        offsets.append(first - start)
        lengths.append(length)
        for kv, cache in enumerate((cache_k, cache_v)):
            copies.append((
                pltpu.make_async_copy(
                    cache.at[slot, pl.ds(start, COPY)], body.at[n, kv], sems.at[n, kv, 0]
                ),
                pltpu.make_async_copy(
                    cache.at[slot, pl.ds(0, ROW_TILE)], sink.at[n, kv], sems.at[n, kv, 1]
                ),
            ))
    for pair in copies:
        for copy in pair:
            copy.start()
    residual_copy.start()
    bias_copy.start()
    weight_copy.start()

    for copy in small[2:]:
        copy.wait()

    row = lax.broadcasted_iota(jnp.int32, (8, width), 0)
    lane = lax.broadcasted_iota(jnp.int32, (8, width), 1)
    own = row == lax.div(lane, HD)
    head_row = lax.broadcasted_iota(jnp.int32, (8, COPY), 0)
    column = lax.broadcasted_iota(jnp.int32, (8, COPY), 1)
    slopes = jnp.zeros((8, COPY), F32)
    for h in range(local_heads):
        slopes = jnp.where(head_row == h, head_slope(local_heads, h), slopes)

    for n, slot in enumerate(slot_of):
        def newest(ref, slot=slot):
            both = ref[...].astype(F32)
            return jnp.where(slot == 0, both[0:1], both[1:2])

        windows = []
        for kv, new in enumerate((new_k, new_v)):
            for copy in copies[2 * n + kv]:
                copy.wait()
            rolled = pltpu.roll(
                body[n, kv].astype(F32), lax.rem(COPY + SINK - offsets[n], COPY), 0
            )
            top = jnp.where(row < SINK, sink[n, kv].astype(F32)[:8], rolled[:8])
            tail = jnp.where(row == SPAN - 1 - WIN, newest(new), rolled[WIN : WIN + 8])
            windows.append(jnp.concatenate([top, rolled[8:WIN], tail, rolled[WIN + 8 :]], axis=0))
        keys, values = (window.astype(BF16) for window in windows)
        query = jnp.where(own, newest(new_q), 0.0).astype(BF16)
        scores = dot(query, keys, ((1,), (1,))) * SCALE
        distance = jnp.where(column < SINK, lengths[n] - column, SPAN - 1 - column).astype(F32)
        scores = jnp.where(column < SPAN, scores - slopes * distance, MASKED)
        terms = jnp.exp2(scores - jnp.max(scores, axis=1, keepdims=True))
        weights = (terms / jnp.sum(terms, axis=1, keepdims=True)).astype(BF16)
        mixed = dot(weights, values, ((1,), (0,)))
        mixed = jnp.sum(jnp.where(own, mixed, 0.0), axis=0, keepdims=True)
        if n == 0:
            window_out[0, 0, :WIN] = keys[:WIN]
            last = jnp.where(row == SPAN - WIN, mixed, windows[0][WIN : WIN + 8])
            window_out[0, 0, WIN:] = last.astype(BF16)
            window_out[0, 1] = values[: WIN + 8]
        else:
            stay_out[...] = mixed.astype(BF16)

    residual_copy.wait()
    bias_copy.wait()
    half = (residual_ref.shape[0] - 2) // 2
    lower, upper = residual_ref[: half + 8].astype(F32), residual_ref[half:].astype(F32)
    upper = jnp.concatenate([upper, jnp.zeros((6, width), F32)], axis=0)
    packed_ref[part : part + half + 8] = jnp.where(side_of() == 0, upper, lower).astype(BF16)
    bias = bias_ref[...]
    high = bias.astype(BF16).astype(F32)
    packed_ref[part + half + 8 :] = jnp.where(row == 0, high, jnp.where(row == 1, bias - high, 0.0)).astype(BF16)
    weight_copy.wait()


def decode(moving, cache_len, new_q, new_k, new_v, cache_k, cache_v, weight, residual, bias):
    width = cache_k.shape[2]
    tail = (residual.shape[0] - 2) // 2 + 16
    return pl.pallas_call(
        decode_kernel,
        name="decode",
        compiler_params=pltpu.CompilerParams(vmem_limit_bytes=ROOM),
        out_shape=(
            placed((1, 2, WIN + 8, width), BF16),
            jax.ShapeDtypeStruct((1, width), BF16),
            kept((weight.shape[0] // 2 + tail, width), BF16),
        ),
        in_specs=[HBM] * 10,
        out_specs=(VMEM,) * 3,
        scratch_shapes=[
            pltpu.SMEM(moving.shape, jnp.int32),
            pltpu.SMEM(cache_len.shape, jnp.int32),
            *[pltpu.VMEM(new_q.shape, BF16)] * 3,
            pltpu.VMEM((2, 2, COPY, width), BF16),
            pltpu.VMEM((2, 2, ROW_TILE, width), BF16),
            pltpu.SemaphoreType.DMA((2, 2, 2)),
            pltpu.SemaphoreType.DMA((5,)),
            pltpu.VMEM(residual.shape, BF16),
            pltpu.VMEM((1, width), F32),
            pltpu.SemaphoreType.DMA((3,)),
        ],
    )(*map(far, (moving, cache_len, new_q, new_k, new_v, cache_k, cache_v, weight, residual, bias)))


def prompt_kernel(
    length_ref, q_ref, k_ref, v_ref, out_hbm, out_ref, sems, *, block,
):
    rows, width = q_ref.shape
    length = length_ref[0]
    copies = []
    for step, first in enumerate(range(0, rows, block)):
        keys = first + block
        query_at = lax.broadcasted_iota(jnp.int32, (block, keys), 0) + first
        key_at = lax.broadcasted_iota(jnp.int32, (block, keys), 1)
        allowed = (key_at <= query_at) & (key_at < length)
        distance = (query_at - key_at).astype(F32)
        for h in range(width // HD):
            cols = slice(h * HD, (h + 1) * HD)
            scores = dot(q_ref[first:keys, cols], k_ref[:keys, cols], ((1,), (1,))) * SCALE
            scores = jnp.where(allowed, scores - head_slope(width // HD, h) * distance, MASKED)
            terms = jnp.exp2(scores - jnp.max(scores, axis=1, keepdims=True))
            weights = (terms / jnp.sum(terms, axis=1, keepdims=True)).astype(BF16)
            out_ref[first:keys, cols] = dot(weights, v_ref[:keys, cols], ((1,), (0,))).astype(BF16)
        for member in range(out_hbm.shape[0]):
            lower = member // 2 % 2 == 0
            if lower and step == 0:
                here, there = slice(0, block), slice(0, block)
            elif lower:
                here, there = slice(block, block + 8), slice(block, block + 8)
            elif step == 1:
                here, there = slice(block, rows), slice(0, block)
            else:
                continue
            copy = pltpu.make_async_copy(out_ref.at[here], out_hbm.at[member, there], sems.at[step, member])
            copy.start()
            copies.append(copy)
    for copy in copies:
        copy.wait()


def prompt(length, q, k, v, members):
    rows, width = q.shape
    block = rows // 2
    return pl.pallas_call(
        functools.partial(prompt_kernel, block=block),
        name="prompt",
        compiler_params=pltpu.CompilerParams(vmem_limit_bytes=ROOM),
        out_shape=placed((members, block + 8, width), BF16),
        in_specs=[SMEM, VMEM, VMEM, VMEM],
        out_specs=HBM,
        scratch_shapes=[
            pltpu.VMEM((rows, width), BF16),
            pltpu.SemaphoreType.DMA((rows // block, members)),
        ],
    )(length, near(q), near(k), near(v))


def insert_kernel(stay_ref, come_ref, given, rows_hbm, tile, sems):
    del given
    row = lax.broadcasted_iota(jnp.int32, tile.shape, 0)
    come = come_ref[0, 0, WIN:].astype(F32)[SPAN - WIN : SPAN - WIN + 1]
    tile[...] = jnp.where(row == 0, stay_ref[...].astype(F32), jnp.where(row == 1, come, 0.0)).astype(BF16)
    members, rows, _ = rows_hbm.shape
    copies = [
        pltpu.make_async_copy(tile, rows_hbm.at[member, pl.ds(rows - 8, 8)], sems.at[member])
        for member in range(members)
        if member // 2 % 2 == 1
    ]
    for copy in copies:
        copy.start()
    for copy in copies:
        copy.wait()


def insert(stay_row, come, rows):
    members, _, width = rows.shape
    return pl.pallas_call(
        insert_kernel,
        name="insert",
        compiler_params=pltpu.CompilerParams(vmem_limit_bytes=ROOM),
        out_shape=placed(rows.shape, rows.dtype),
        in_specs=[VMEM, VMEM, HBM],
        out_specs=HBM,
        scratch_shapes=[pltpu.VMEM((8, width), BF16), pltpu.SemaphoreType.DMA((members,))],
        input_output_aliases={2: 0},
    )(stay_row, near(come), far(rows))


def project_kernel(
    x_ref, w_ref, packed_ref, swapped_ref, bias_ref, residual_hbm,
    own_hbm, pair_hbm, stats_ref, residual_ref, own_ref, pair_ref, sems,
):
    residual_copy = pltpu.make_async_copy(residual_hbm, residual_ref, sems.at[0])
    residual_copy.start()
    sources, rows, width = x_ref.shape
    part = sources // 2
    core, side = core_of(), side_of()
    near_half, far_half = core * part, (1 - core) * part
    blocks = [slice(start, min(start + BLOCK, rows)) for start in range(0, rows, BLOCK)]
    for at in blocks:
        pair_ref[at] = sum(
            dot(x_ref[near_half + s, at], packed_ref[s * width : (s + 1) * width], ((1,), (0,)))
            + dot(x_ref[far_half + s, at], swapped_ref[s * width : (s + 1) * width], ((1,), (0,)))
            for s in range(part)
        )
        own_ref[at] = sum(
            dot(x_ref[s, at], w_ref[s * width : (s + 1) * width], ((1,), (0,))) for s in range(sources)
        )
    residual_copy.wait()
    extra = part * width
    pair_bias = packed_ref[extra + rows :].astype(F32)
    pair_bias = pair_bias[0:1] + pair_bias[1:2]
    copies = []
    for step, at in enumerate(blocks):
        size = at.stop - at.start
        upper = residual_ref[at.start + rows - 8 : min(at.stop + rows - 8, residual_ref.shape[0])].astype(F32)
        if upper.shape[0] < size:
            upper = jnp.concatenate([upper, jnp.zeros((size - upper.shape[0], width), F32)], axis=0)
        own = own_ref[at] + bias_ref[...] + jnp.where(side == 0, residual_ref[at].astype(F32), upper)
        pair = pair_ref[at] + pair_bias + packed_ref[extra + at.start : extra + at.stop].astype(F32)
        own_ref[at] = own
        pair_ref[at] = pair
        for k, (source, target) in enumerate(((own_ref, own_hbm), (pair_ref, pair_hbm))):
            copy = pltpu.make_async_copy(source.at[at], target.at[at], sems.at[1 + 2 * step + k])
            copy.start()
            copies.append(copy)
        mean = jnp.sum(own + pair, axis=1, keepdims=True) * (0.5 / width)
        own_centered, pair_centered = own - mean, pair - mean
        spread = jnp.sum(
            own_centered * own_centered + pair_centered * pair_centered, axis=1, keepdims=True
        )
        lane = lax.broadcasted_iota(jnp.int32, (size, HD), 1)
        table = jnp.where(lane == 0, mean, jnp.where(lane == 1, spread, 0.0))
        stats = table.T[:2]
        for member in range(stats_ref.shape[0]):
            stats_ref[member, :, at] = stats
    for copy in copies:
        copy.wait()


def project(gathered, weight, packed, swapped, bias, residual):
    sources, rows, width = gathered.shape
    steps = -(-rows // BLOCK)
    return pl.pallas_call(
        project_kernel,
        name="project",
        compiler_params=pltpu.CompilerParams(vmem_limit_bytes=ROOM),
        out_shape=(
            placed((rows, width), F32),
            placed((rows, width), F32),
            placed((sources, 2, rows), F32),
        ),
        in_specs=[VMEM] * 5 + [HBM],
        out_specs=(HBM, HBM, VMEM),
        scratch_shapes=[
            pltpu.VMEM(residual.shape, BF16),
            pltpu.VMEM((rows, width), F32),
            pltpu.VMEM((rows, width), F32),
            pltpu.SemaphoreType.DMA((1 + 2 * steps,)),
        ],
    )(near(gathered), near(weight), near(packed), near(swapped), bias, far(residual))


def norm_kernel(
    stats_ref, own_hbm, come_ref, gain_ref, shift_ref, hidden_ref, normed_ref, own_ref, sem,
):
    copy = pltpu.make_async_copy(own_hbm, own_ref, sem)
    copy.start()
    members = stats_ref.shape[0]
    rows, width = own_ref.shape
    parts = members // 2
    side = side_of()
    tables = []
    for half in range(2):
        sources = [s for s in range(members) if s // 2 % 2 == half]
        means = [stats_ref[s, 0:1, :] for s in sources]
        mean = sum(means) * (1.0 / parts)
        spread = sum(
            stats_ref[s, 1:2, :] + (2 * width) * ((part - mean) * (part - mean))
            for s, part in zip(sources, means)
        )
        scale = lax.rsqrt(spread * (1.0 / (members * width)) + EPSILON)
        row = lax.broadcasted_iota(jnp.int32, (8, rows), 0)
        tables.append(jnp.where(row == 0, mean, jnp.where(row == 1, scale, 0.0)))
    copy.wait()
    total = hidden_ref.shape[0]
    for half, table in enumerate(tables):
        first = half * (rows - 8)
        used = rows - 8 if half == 0 else total - first
        for start in range(0, used, BLOCK):
            at = slice(start, min(start + BLOCK, used))
            columns = table[:, at].T
            own, come = own_ref[at], come_ref[at]
            stream = jnp.where(side == half, own, come)
            to = slice(first + at.start, first + at.stop)
            hidden_ref[to] = stream.astype(BF16)
            normed_ref[to] = (
                (stream - columns[:, 0:1]) * columns[:, 1:2] * gain_ref[...] + shift_ref[...]
            ).astype(BF16)


def norm(stats, own, come, gain, shift, rows):
    out = jax.ShapeDtypeStruct((rows, own.shape[1]), BF16)
    return pl.pallas_call(
        norm_kernel,
        name="norm",
        compiler_params=pltpu.CompilerParams(vmem_limit_bytes=ROOM),
        out_shape=(out, out),
        in_specs=[VMEM, HBM, VMEM, VMEM, VMEM],
        out_specs=(VMEM, VMEM),
        scratch_shapes=[pltpu.VMEM(own.shape, F32), pltpu.SemaphoreType.DMA],
    )(near(stats), far(own), near(come), gain, shift)


def to_partner(block):
    count = lax.axis_size("rep")
    return lax.ppermute(block, "rep", [(i, (i + count // 2) % count) for i in range(count)])


def to_pair(block):
    return lax.ppermute(block, "tp", [(i, i ^ 2) for i in range(lax.axis_size("tp"))])


def to_sibling(block):
    return lax.ppermute(block, "rep", [(i, i ^ 1) for i in range(lax.axis_size("rep"))])


def exchange(blocks):
    return lax.all_to_all(blocks, "tp", 0, 0)


def after(values, other):
    return lax.optimization_barrier((values, other))[0]


def on_device(
    prompt_q, prompt_k, prompt_v, prompt_len, cache_keys, cache_values, new_q, new_k, new_v,
    cache_len, moving, out_weight, out_bias, residual, ln_gain, ln_shift,
):
    window, stay_row, packed = decode(
        moving, cache_len, new_q, new_k, new_v, cache_keys, cache_values, out_weight, residual, out_bias[None]
    )
    come = to_partner(window)
    packed = to_pair(packed)
    swapped = to_sibling(packed)
    mixed = prompt(prompt_len, prompt_q, prompt_k, prompt_v, lax.axis_size("tp"))
    mixed = insert(stay_row, come, mixed)
    moved_window = come[:, :, :SPAN]
    own, pair, stats = project(
        exchange(mixed), out_weight, packed, swapped, out_bias[None], residual
    )
    stats = exchange(stats)
    hidden_out, normed = norm(
        stats, own, to_pair(pair), ln_gain[None], ln_shift[None], residual.shape[0]
    )
    return (hidden_out, normed, moved_window)


def solution(mesh):
    in_specs = (
        P("rep", "tp"), P("rep", "tp"), P("rep", "tp"), P("rep"),
        P("rep", None, "tp"), P("rep", None, "tp"),
        P("rep", "tp"), P("rep", "tp"), P("rep", "tp"),
        P(), P(), P(None, "tp"), P("tp"), P("rep", "tp"), P("tp"), P("tp"),
    )
    out_specs = (P("rep", "tp"), P("rep", "tp"), P("rep", None, None, "tp"))
    return jax.shard_map(
        on_device, mesh=mesh, in_specs=in_specs, out_specs=out_specs, check_vma=False
    )
```

```python
import functools
import math

import jax
import jax.numpy as jnp
from jax import lax
from jax.experimental import pallas as pl
from jax.experimental.pallas import tpu as pltpu
from jax.sharding import PartitionSpec as P

D = 2048
HEADS = 16
HD = 128
SINK = 4
WIN = 256
SPAN = SINK + WIN
ROW_TILE = 16
COPY = 272

LOG2E = math.log2(math.e)
SCALE = LOG2E / math.sqrt(HD)
MASKED = -1e30
EPSILON = 1e-05
BLOCK = 128
ROOM = 16 * 2**20

F32 = jnp.float32
BF16 = jnp.bfloat16
HIGHEST = lax.Precision.HIGHEST

SMEM = pl.BlockSpec(memory_space=pltpu.SMEM)
VMEM = pl.BlockSpec(memory_space=pltpu.VMEM)
HBM = pl.BlockSpec(memory_space=pl.ANY)


def kept(shape, dtype):
    return pltpu.VMEM(shape, dtype)


def placed(shape, dtype):
    return pltpu.HBM(shape, dtype)


def near(array):
    return pltpu.with_memory_space_constraint(array, pltpu.VMEM)


def far(array):
    return pltpu.with_memory_space_constraint(array, pltpu.HBM)


def dot(a, b, contract, precision=None):
    return lax.dot_general(a, b, (contract, ((), ())), precision=precision, preferred_element_type=F32)


def core_of():
    return lax.rem(lax.axis_index("rep"), 2)


def side_of():
    return lax.rem(lax.div(lax.axis_index("tp"), 2), 2)


def head_slope(local_heads, head):
    tp = lax.axis_index("tp")
    slope = jnp.float32(LOG2E * 2.0 ** (-8.0 * (head + 1) / HEADS))
    step = 2.0 ** (-8.0 * local_heads / HEADS)
    for k in range(1, HEADS // local_heads):
        slope = jnp.where(tp >= k, slope * step, slope)
    return slope


def decode_kernel(
    moving_hbm, cache_len_hbm, new_q_hbm, new_k_hbm, new_v_hbm, cache_k, cache_v, weight_hbm, residual_hbm, bias_hbm,
    window_out, stay_out, packed_ref,
    moving, cache_len, new_q, new_k, new_v, body, sink, sems, small_sems, residual_ref, bias_ref, pack_sems,
):
    part = weight_hbm.shape[0] // 2
    weight_copy = pltpu.make_async_copy(
        weight_hbm.at[pl.ds(pl.multiple_of(core_of() * part, part), part)],
        packed_ref.at[pl.ds(0, part)],
        pack_sems.at[0],
    )
    residual_copy = pltpu.make_async_copy(residual_hbm, residual_ref, pack_sems.at[1])
    bias_copy = pltpu.make_async_copy(bias_hbm, bias_ref, pack_sems.at[2])
    small = [
        pltpu.make_async_copy(source, target, small_sems.at[i])
        for i, (source, target) in enumerate((
            (moving_hbm, moving), (cache_len_hbm, cache_len),
            (new_q_hbm, new_q), (new_k_hbm, new_k), (new_v_hbm, new_v),
        ))
    ]
    for copy in small:
        copy.start()
    small[0].wait()
    small[1].wait()
    rep = lax.axis_index("rep")
    slots, capacity, width = cache_k.shape
    local_heads = width // HD
    leaving = moving[rep]
    slot_of = (leaving, 1 - leaving)
    copies = []
    offsets, lengths = [], []
    for n, slot in enumerate(slot_of):
        length = cache_len[rep * slots + slot]
        first = length + 1 - WIN
        start = pl.multiple_of(
            jnp.minimum(lax.div(first, ROW_TILE) * ROW_TILE, capacity - COPY), ROW_TILE
        )
        offsets.append(first - start)
        lengths.append(length)
        for kv, cache in enumerate((cache_k, cache_v)):
            copies.append((
                pltpu.make_async_copy(
                    cache.at[slot, pl.ds(start, COPY)], body.at[n, kv], sems.at[n, kv, 0]
                ),
                pltpu.make_async_copy(
                    cache.at[slot, pl.ds(0, ROW_TILE)], sink.at[n, kv], sems.at[n, kv, 1]
                ),
            ))
    for pair in copies:
        for copy in pair:
            copy.start()
    residual_copy.start()
    bias_copy.start()
    weight_copy.start()

    for copy in small[2:]:
        copy.wait()

    row = lax.broadcasted_iota(jnp.int32, (8, width), 0)
    lane = lax.broadcasted_iota(jnp.int32, (8, width), 1)
    own = row == lax.div(lane, HD)
    head_row = lax.broadcasted_iota(jnp.int32, (8, COPY), 0)
    column = lax.broadcasted_iota(jnp.int32, (8, COPY), 1)
    slopes = jnp.zeros((8, COPY), F32)
    for h in range(local_heads):
        slopes = jnp.where(head_row == h, head_slope(local_heads, h), slopes)

    for n, slot in enumerate(slot_of):
        def newest(ref, slot=slot):
            both = ref[...].astype(F32)
            return jnp.where(slot == 0, both[0:1], both[1:2])

        windows = []
        for kv, new in enumerate((new_k, new_v)):
            for copy in copies[2 * n + kv]:
                copy.wait()
            rolled = pltpu.roll(
                body[n, kv].astype(F32), lax.rem(COPY + SINK - offsets[n], COPY), 0
            )
            top = jnp.where(row < SINK, sink[n, kv].astype(F32)[:8], rolled[:8])
            tail = jnp.where(row == SPAN - 1 - WIN, newest(new), rolled[WIN : WIN + 8])
            windows.append(jnp.concatenate([top, rolled[8:WIN], tail, rolled[WIN + 8 :]], axis=0))
        keys, values = (window.astype(BF16) for window in windows)
        query = jnp.where(own, newest(new_q), 0.0).astype(BF16)
        scores = dot(query, keys, ((1,), (1,))) * SCALE
        distance = jnp.where(column < SINK, lengths[n] - column, SPAN - 1 - column).astype(F32)
        scores = jnp.where(column < SPAN, scores - slopes * distance, MASKED)
        terms = jnp.exp2(scores - jnp.max(scores, axis=1, keepdims=True))
        weights = (terms / jnp.sum(terms, axis=1, keepdims=True)).astype(BF16)
        mixed = dot(weights, values, ((1,), (0,)))
        mixed = jnp.sum(jnp.where(own, mixed, 0.0), axis=0, keepdims=True)
        if n == 0:
            window_out[0, 0, :WIN] = keys[:WIN]
            last = jnp.where(row == SPAN - WIN, mixed, windows[0][WIN : WIN + 8])
            window_out[0, 0, WIN:] = last.astype(BF16)
            window_out[0, 1] = values[: WIN + 8]
        else:
            stay_out[...] = mixed.astype(BF16)

    residual_copy.wait()
    bias_copy.wait()
    half = (residual_ref.shape[0] - 2) // 2
    lower, upper = residual_ref[: half + 8].astype(F32), residual_ref[half:].astype(F32)
    upper = jnp.concatenate([upper, jnp.zeros((6, width), F32)], axis=0)
    packed_ref[part : part + half + 8] = jnp.where(side_of() == 0, upper, lower).astype(BF16)
    bias = bias_ref[...]
    high = bias.astype(BF16).astype(F32)
    packed_ref[part + half + 8 :] = jnp.where(row == 0, high, jnp.where(row == 1, bias - high, 0.0)).astype(BF16)
    weight_copy.wait()


def decode(moving, cache_len, new_q, new_k, new_v, cache_k, cache_v, weight, residual, bias):
    width = cache_k.shape[2]
    tail = (residual.shape[0] - 2) // 2 + 16
    return pl.pallas_call(
        decode_kernel,
        name="decode",
        compiler_params=pltpu.CompilerParams(vmem_limit_bytes=ROOM),
        out_shape=(
            placed((1, 2, WIN + 8, width), BF16),
            jax.ShapeDtypeStruct((1, width), BF16),
            kept((weight.shape[0] // 2 + tail, width), BF16),
        ),
        in_specs=[HBM] * 10,
        out_specs=(VMEM,) * 3,
        scratch_shapes=[
            pltpu.SMEM(moving.shape, jnp.int32),
            pltpu.SMEM(cache_len.shape, jnp.int32),
            *[pltpu.VMEM(new_q.shape, BF16)] * 3,
            pltpu.VMEM((2, 2, COPY, width), BF16),
            pltpu.VMEM((2, 2, ROW_TILE, width), BF16),
            pltpu.SemaphoreType.DMA((2, 2, 2)),
            pltpu.SemaphoreType.DMA((5,)),
            pltpu.VMEM(residual.shape, BF16),
            pltpu.VMEM((1, width), F32),
            pltpu.SemaphoreType.DMA((3,)),
        ],
    )(*map(far, (moving, cache_len, new_q, new_k, new_v, cache_k, cache_v, weight, residual, bias)))


def prompt_kernel(
    length_ref, q_ref, k_ref, v_ref, out_hbm, out_ref, sems, *, block,
):
    rows, width = q_ref.shape
    length = length_ref[0]
    copies = []
    for step, first in enumerate(range(0, rows, block)):
        keys = first + block
        query_at = lax.broadcasted_iota(jnp.int32, (block, keys), 0) + first
        key_at = lax.broadcasted_iota(jnp.int32, (block, keys), 1)
        allowed = (key_at <= query_at) & (key_at < length)
        distance = (query_at - key_at).astype(F32)
        for h in range(width // HD):
            cols = slice(h * HD, (h + 1) * HD)
            scores = dot(q_ref[first:keys, cols], k_ref[:keys, cols], ((1,), (1,))) * SCALE
            scores = jnp.where(allowed, scores - head_slope(width // HD, h) * distance, MASKED)
            terms = jnp.exp2(scores - jnp.max(scores, axis=1, keepdims=True))
            weights = (terms / jnp.sum(terms, axis=1, keepdims=True)).astype(BF16)
            out_ref[first:keys, cols] = dot(weights, v_ref[:keys, cols], ((1,), (0,))).astype(BF16)
        for member in range(out_hbm.shape[0]):
            lower = member // 2 % 2 == 0
            if lower and step == 0:
                here, there = slice(0, block), slice(0, block)
            elif lower:
                here, there = slice(block, block + 8), slice(block, block + 8)
            elif step == 1:
                here, there = slice(block, rows), slice(0, block)
            else:
                continue
            copy = pltpu.make_async_copy(out_ref.at[here], out_hbm.at[member, there], sems.at[step, member])
            copy.start()
            copies.append(copy)
    for copy in copies:
        copy.wait()


def prompt(length, q, k, v, members):
    rows, width = q.shape
    block = rows // 2
    return pl.pallas_call(
        functools.partial(prompt_kernel, block=block),
        name="prompt",
        compiler_params=pltpu.CompilerParams(vmem_limit_bytes=ROOM),
        out_shape=placed((members, block + 8, width), BF16),
        in_specs=[SMEM, VMEM, VMEM, VMEM],
        out_specs=HBM,
        scratch_shapes=[
            pltpu.VMEM((rows, width), BF16),
            pltpu.SemaphoreType.DMA((rows // block, members)),
        ],
    )(length, near(q), near(k), near(v))


def insert_kernel(stay_ref, come_ref, given, rows_hbm, tile, sems):
    del given
    row = lax.broadcasted_iota(jnp.int32, tile.shape, 0)
    come = come_ref[0, 0, WIN:].astype(F32)[SPAN - WIN : SPAN - WIN + 1]
    tile[...] = jnp.where(row == 0, stay_ref[...].astype(F32), jnp.where(row == 1, come, 0.0)).astype(BF16)
    members, rows, _ = rows_hbm.shape
    copies = [
        pltpu.make_async_copy(tile, rows_hbm.at[member, pl.ds(rows - 8, 8)], sems.at[member])
        for member in range(members)
        if member // 2 % 2 == 1
    ]
    for copy in copies:
        copy.start()
    for copy in copies:
        copy.wait()


def insert(stay_row, come, rows):
    members, _, width = rows.shape
    return pl.pallas_call(
        insert_kernel,
        name="insert",
        compiler_params=pltpu.CompilerParams(vmem_limit_bytes=ROOM),
        out_shape=placed(rows.shape, rows.dtype),
        in_specs=[VMEM, VMEM, HBM],
        out_specs=HBM,
        scratch_shapes=[pltpu.VMEM((8, width), BF16), pltpu.SemaphoreType.DMA((members,))],
        input_output_aliases={2: 0},
    )(stay_row, near(come), far(rows))


def project_kernel(
    x_ref, w_ref, packed_ref, swapped_ref, bias_ref, residual_hbm,
    own_hbm, pair_hbm, stats_ref, residual_ref, own_ref, pair_ref, sems,
):
    residual_copy = pltpu.make_async_copy(residual_hbm, residual_ref, sems.at[0])
    residual_copy.start()
    sources, rows, width = x_ref.shape
    part = sources // 2
    core, side = core_of(), side_of()
    near_half, far_half = core * part, (1 - core) * part
    blocks = [slice(start, min(start + BLOCK, rows)) for start in range(0, rows, BLOCK)]
    for at in blocks:
        pair_ref[at] = sum(
            dot(x_ref[near_half + s, at], packed_ref[s * width : (s + 1) * width], ((1,), (0,)))
            + dot(x_ref[far_half + s, at], swapped_ref[s * width : (s + 1) * width], ((1,), (0,)))
            for s in range(part)
        )
        own_ref[at] = sum(
            dot(x_ref[s, at], w_ref[s * width : (s + 1) * width], ((1,), (0,))) for s in range(sources)
        )
    residual_copy.wait()
    extra = part * width
    pair_bias = packed_ref[extra + rows :].astype(F32)
    pair_bias = pair_bias[0:1] + pair_bias[1:2]
    copies = []
    for step, at in enumerate(blocks):
        size = at.stop - at.start
        upper = residual_ref[at.start + rows - 8 : min(at.stop + rows - 8, residual_ref.shape[0])].astype(F32)
        if upper.shape[0] < size:
            upper = jnp.concatenate([upper, jnp.zeros((size - upper.shape[0], width), F32)], axis=0)
        own = own_ref[at] + bias_ref[...] + jnp.where(side == 0, residual_ref[at].astype(F32), upper)
        pair = pair_ref[at] + pair_bias + packed_ref[extra + at.start : extra + at.stop].astype(F32)
        own_ref[at] = own
        pair_ref[at] = pair
        for k, (source, target) in enumerate(((own_ref, own_hbm), (pair_ref, pair_hbm))):
            copy = pltpu.make_async_copy(source.at[at], target.at[at], sems.at[1 + 2 * step + k])
            copy.start()
            copies.append(copy)
        mean = jnp.sum(own + pair, axis=1, keepdims=True) * (0.5 / width)
        own_centered, pair_centered = own - mean, pair - mean
        spread = jnp.sum(
            own_centered * own_centered + pair_centered * pair_centered, axis=1, keepdims=True
        )
        lane = lax.broadcasted_iota(jnp.int32, (size, HD), 1)
        table = jnp.where(lane == 0, mean, jnp.where(lane == 1, spread, 0.0))
        stats = table.T[:2]
        for member in range(stats_ref.shape[0]):
            stats_ref[member, :, at] = stats
    for copy in copies:
        copy.wait()


def project(gathered, weight, packed, swapped, bias, residual):
    sources, rows, width = gathered.shape
    steps = -(-rows // BLOCK)
    return pl.pallas_call(
        project_kernel,
        name="project",
        compiler_params=pltpu.CompilerParams(vmem_limit_bytes=ROOM),
        out_shape=(
            placed((rows, width), F32),
            placed((rows, width), F32),
            placed((sources, 2, rows), F32),
        ),
        in_specs=[VMEM] * 5 + [HBM],
        out_specs=(HBM, HBM, VMEM),
        scratch_shapes=[
            pltpu.VMEM(residual.shape, BF16),
            pltpu.VMEM((rows, width), F32),
            pltpu.VMEM((rows, width), F32),
            pltpu.SemaphoreType.DMA((1 + 2 * steps,)),
        ],
    )(near(gathered), near(weight), near(packed), near(swapped), bias, far(residual))


def tables_kernel(stats_ref, out_ref, *, width):
    members, _, rows = stats_ref.shape
    parts = members // 2
    row = lax.broadcasted_iota(jnp.int32, (8, rows), 0)
    for half in range(2):
        sources = [s for s in range(members) if s // 2 % 2 == half]
        means = [stats_ref[s, 0:1, :] for s in sources]
        mean = sum(means) * (1.0 / parts)
        spread = sum(
            stats_ref[s, 1:2, :] + (2 * width) * ((part - mean) * (part - mean))
            for s, part in zip(sources, means)
        )
        scale = lax.rsqrt(spread * (1.0 / (members * width)) + EPSILON)
        out_ref[half] = jnp.where(row == 0, mean, jnp.where(row == 1, scale, 0.0))


def tables(stats, width):
    return pl.pallas_call(
        functools.partial(tables_kernel, width=width),
        name="tables",
        cost_estimate=pl.CostEstimate(flops=8 * 10**9, bytes_accessed=2**20, transcendentals=0),
        compiler_params=pltpu.CompilerParams(vmem_limit_bytes=ROOM),
        out_shape=kept((2, 8, stats.shape[2]), F32),
        in_specs=[VMEM],
        out_specs=VMEM,
    )(near(stats))


def norm_kernel(
    tables_ref, own_hbm, come_ref, gain_ref, shift_ref, hidden_ref, normed_ref, own_ref, sem,
):
    copy = pltpu.make_async_copy(own_hbm, own_ref, sem)
    copy.start()
    copy.wait()
    rows, width = own_ref.shape
    side = side_of()
    total = hidden_ref.shape[0]
    for half in range(2):
        first = half * (rows - 8)
        used = rows - 8 if half == 0 else total - first
        for start in range(0, used, BLOCK):
            at = slice(start, min(start + BLOCK, used))
            columns = tables_ref[half, :, at].T
            own, come = own_ref[at], come_ref[at]
            stream = jnp.where(side == half, own, come)
            to = slice(first + at.start, first + at.stop)
            hidden_ref[to] = stream.astype(BF16)
            normed_ref[to] = (
                (stream - columns[:, 0:1]) * columns[:, 1:2] * gain_ref[...] + shift_ref[...]
            ).astype(BF16)


def norm(scales, own, come, gain, shift, rows):
    out = jax.ShapeDtypeStruct((rows, own.shape[1]), BF16)
    return pl.pallas_call(
        norm_kernel,
        name="norm",
        compiler_params=pltpu.CompilerParams(vmem_limit_bytes=ROOM),
        out_shape=(out, out),
        in_specs=[VMEM, HBM, VMEM, VMEM, VMEM],
        out_specs=(VMEM, VMEM),
        scratch_shapes=[pltpu.VMEM(own.shape, F32), pltpu.SemaphoreType.DMA],
    )(near(scales), far(own), near(come), gain, shift)


def to_partner(block):
    count = lax.axis_size("rep")
    return lax.ppermute(block, "rep", [(i, (i + count // 2) % count) for i in range(count)])


def to_pair(block):
    return lax.ppermute(block, "tp", [(i, i ^ 2) for i in range(lax.axis_size("tp"))])


def to_sibling(block):
    return lax.ppermute(block, "rep", [(i, i ^ 1) for i in range(lax.axis_size("rep"))])


def exchange(blocks):
    return lax.all_to_all(blocks, "tp", 0, 0)


def after(values, other):
    return lax.optimization_barrier((values, other))[0]


def on_device(
    prompt_q, prompt_k, prompt_v, prompt_len, cache_keys, cache_values, new_q, new_k, new_v,
    cache_len, moving, out_weight, out_bias, residual, ln_gain, ln_shift,
):
    window, stay_row, packed = decode(
        moving, cache_len, new_q, new_k, new_v, cache_keys, cache_values, out_weight, residual, out_bias[None]
    )
    come = to_partner(window)
    packed = to_pair(packed)
    swapped = to_sibling(packed)
    mixed = prompt(prompt_len, prompt_q, prompt_k, prompt_v, lax.axis_size("tp"))
    mixed = insert(stay_row, come, mixed)
    moved_window = come[:, :, :SPAN]
    own, pair, stats = project(
        exchange(mixed), out_weight, packed, swapped, out_bias[None], residual
    )
    scales = tables(exchange(stats), own.shape[1])
    hidden_out, normed = norm(
        scales, own, to_pair(pair), ln_gain[None], ln_shift[None], residual.shape[0]
    )
    return (hidden_out, normed, moved_window)


def solution(mesh):
    in_specs = (
        P("rep", "tp"), P("rep", "tp"), P("rep", "tp"), P("rep"),
        P("rep", None, "tp"), P("rep", None, "tp"),
        P("rep", "tp"), P("rep", "tp"), P("rep", "tp"),
        P(), P(), P(None, "tp"), P("tp"), P("rep", "tp"), P("tp"), P("tp"),
    )
    out_specs = (P("rep", "tp"), P("rep", "tp"), P("rep", None, None, "tp"))
    return jax.shard_map(
        on_device, mesh=mesh, in_specs=in_specs, out_specs=out_specs, check_vma=False
    )
```

```python
import functools
import math

import jax
import jax.numpy as jnp
from jax import lax
from jax.experimental import pallas as pl
from jax.experimental.layout import Layout, with_layout_constraint
from jax.experimental.pallas import tpu as pltpu
from jax.sharding import PartitionSpec as P

D = 2048
HEADS = 16
HD = 128
SINK = 4
WIN = 256
SPAN = SINK + WIN
ROW_TILE = 16
COPY = 272

LOG2E = math.log2(math.e)
SCALE = LOG2E / math.sqrt(HD)
MASKED = -1e30
EPSILON = 1e-05
BLOCK = 128
ROOM = 16 * 2**20

F32 = jnp.float32
BF16 = jnp.bfloat16
HIGHEST = lax.Precision.HIGHEST

SMEM = pl.BlockSpec(memory_space=pltpu.SMEM)
VMEM = pl.BlockSpec(memory_space=pltpu.VMEM)
HBM = pl.BlockSpec(memory_space=pl.ANY)


def kept(shape, dtype):
    return pltpu.VMEM(shape, dtype)


def placed(shape, dtype):
    return pltpu.HBM(shape, dtype)


def near(array):
    return pltpu.with_memory_space_constraint(array, pltpu.VMEM)


def far(array):
    return pltpu.with_memory_space_constraint(array, pltpu.HBM)


def dot(a, b, contract, precision=None):
    return lax.dot_general(a, b, (contract, ((), ())), precision=precision, preferred_element_type=F32)


def core_of():
    return lax.rem(lax.axis_index("rep"), 2)


def side_of():
    return lax.rem(lax.div(lax.axis_index("tp"), 2), 2)


def head_slope(local_heads, head):
    tp = lax.axis_index("tp")
    slope = jnp.float32(LOG2E * 2.0 ** (-8.0 * (head + 1) / HEADS))
    step = 2.0 ** (-8.0 * local_heads / HEADS)
    for k in range(1, HEADS // local_heads):
        slope = jnp.where(tp >= k, slope * step, slope)
    return slope


def decode_kernel(
    moving_hbm, cache_len_hbm, new_q_hbm, new_k_hbm, new_v_hbm, cache_k, cache_v, weight_hbm, residual_hbm, bias_hbm,
    window_out, stay_out, packed_ref,
    moving, cache_len, new_q, new_k, new_v, body, sink, sems, small_sems, residual_ref, bias_ref, pack_sems,
):
    part = weight_hbm.shape[0] // 2
    weight_copy = pltpu.make_async_copy(
        weight_hbm.at[pl.ds(pl.multiple_of(core_of() * part, part), part)],
        packed_ref.at[pl.ds(0, part)],
        pack_sems.at[0],
    )
    residual_copy = pltpu.make_async_copy(residual_hbm, residual_ref, pack_sems.at[1])
    bias_copy = pltpu.make_async_copy(bias_hbm, bias_ref, pack_sems.at[2])
    small = [
        pltpu.make_async_copy(source, target, small_sems.at[i])
        for i, (source, target) in enumerate((
            (moving_hbm, moving), (cache_len_hbm, cache_len),
            (new_q_hbm, new_q), (new_k_hbm, new_k), (new_v_hbm, new_v),
        ))
    ]
    for copy in small:
        copy.start()
    small[0].wait()
    small[1].wait()
    rep = lax.axis_index("rep")
    slots, capacity, width = cache_k.shape
    local_heads = width // HD
    leaving = moving[rep]
    slot_of = (leaving, 1 - leaving)
    copies = []
    offsets, lengths = [], []
    for n, slot in enumerate(slot_of):
        length = cache_len[rep * slots + slot]
        first = length + 1 - WIN
        start = pl.multiple_of(
            jnp.minimum(lax.div(first, ROW_TILE) * ROW_TILE, capacity - COPY), ROW_TILE
        )
        offsets.append(first - start)
        lengths.append(length)
        for kv, cache in enumerate((cache_k, cache_v)):
            copies.append((
                pltpu.make_async_copy(
                    cache.at[slot, pl.ds(start, COPY)], body.at[n, kv], sems.at[n, kv, 0]
                ),
                pltpu.make_async_copy(
                    cache.at[slot, pl.ds(0, ROW_TILE)], sink.at[n, kv], sems.at[n, kv, 1]
                ),
            ))
    for pair in copies:
        for copy in pair:
            copy.start()
    residual_copy.start()
    bias_copy.start()
    weight_copy.start()

    for copy in small[2:]:
        copy.wait()

    row = lax.broadcasted_iota(jnp.int32, (8, width), 0)
    lane = lax.broadcasted_iota(jnp.int32, (8, width), 1)
    own = row == lax.div(lane, HD)
    head_row = lax.broadcasted_iota(jnp.int32, (8, COPY), 0)
    column = lax.broadcasted_iota(jnp.int32, (8, COPY), 1)
    slopes = jnp.zeros((8, COPY), F32)
    for h in range(local_heads):
        slopes = jnp.where(head_row == h, head_slope(local_heads, h), slopes)

    for n, slot in enumerate(slot_of):
        def newest(ref, slot=slot):
            both = ref[...].astype(F32)
            return jnp.where(slot == 0, both[0:1], both[1:2])

        windows = []
        for kv, new in enumerate((new_k, new_v)):
            for copy in copies[2 * n + kv]:
                copy.wait()
            rolled = pltpu.roll(
                body[n, kv].astype(F32), lax.rem(COPY + SINK - offsets[n], COPY), 0
            )
            top = jnp.where(row < SINK, sink[n, kv].astype(F32)[:8], rolled[:8])
            tail = jnp.where(row == SPAN - 1 - WIN, newest(new), rolled[WIN : WIN + 8])
            windows.append(jnp.concatenate([top, rolled[8:WIN], tail, rolled[WIN + 8 :]], axis=0))
        keys, values = (window.astype(BF16) for window in windows)
        query = jnp.where(own, newest(new_q), 0.0).astype(BF16)
        scores = dot(query, keys, ((1,), (1,))) * SCALE
        distance = jnp.where(column < SINK, lengths[n] - column, SPAN - 1 - column).astype(F32)
        scores = jnp.where(column < SPAN, scores - slopes * distance, MASKED)
        terms = jnp.exp2(scores - jnp.max(scores, axis=1, keepdims=True))
        weights = (terms / jnp.sum(terms, axis=1, keepdims=True)).astype(BF16)
        mixed = dot(weights, values, ((1,), (0,)))
        mixed = jnp.sum(jnp.where(own, mixed, 0.0), axis=0, keepdims=True)
        if n == 0:
            window_out[0, 0, :WIN] = keys[:WIN]
            last = jnp.where(row == SPAN - WIN, mixed, windows[0][WIN : WIN + 8])
            window_out[0, 0, WIN:] = last.astype(BF16)
            window_out[0, 1] = values[: WIN + 8]
        else:
            stay_out[...] = mixed.astype(BF16)

    residual_copy.wait()
    bias_copy.wait()
    half = (residual_ref.shape[0] - 2) // 2
    lower, upper = residual_ref[: half + 8].astype(F32), residual_ref[half:].astype(F32)
    upper = jnp.concatenate([upper, jnp.zeros((6, width), F32)], axis=0)
    packed_ref[part : part + half + 8] = jnp.where(side_of() == 0, upper, lower).astype(BF16)
    bias = bias_ref[...]
    high = bias.astype(BF16).astype(F32)
    packed_ref[part + half + 8 :] = jnp.where(row == 0, high, jnp.where(row == 1, bias - high, 0.0)).astype(BF16)
    weight_copy.wait()


def decode(moving, cache_len, new_q, new_k, new_v, cache_k, cache_v, weight, residual, bias):
    width = cache_k.shape[2]
    tail = (residual.shape[0] - 2) // 2 + 16
    return pl.pallas_call(
        decode_kernel,
        name="decode",
        compiler_params=pltpu.CompilerParams(vmem_limit_bytes=ROOM),
        out_shape=(
            placed((1, 2, WIN + 8, width), BF16),
            jax.ShapeDtypeStruct((1, width), BF16),
            kept((weight.shape[0] // 2 + tail, width), BF16),
        ),
        in_specs=[HBM] * 10,
        out_specs=(VMEM,) * 3,
        scratch_shapes=[
            pltpu.SMEM(moving.shape, jnp.int32),
            pltpu.SMEM(cache_len.shape, jnp.int32),
            *[pltpu.VMEM(new_q.shape, BF16)] * 3,
            pltpu.VMEM((2, 2, COPY, width), BF16),
            pltpu.VMEM((2, 2, ROW_TILE, width), BF16),
            pltpu.SemaphoreType.DMA((2, 2, 2)),
            pltpu.SemaphoreType.DMA((5,)),
            pltpu.VMEM(residual.shape, BF16),
            pltpu.VMEM((1, width), F32),
            pltpu.SemaphoreType.DMA((3,)),
        ],
    )(*map(far, (moving, cache_len, new_q, new_k, new_v, cache_k, cache_v, weight, residual, bias)))


def prompt_kernel(
    length_ref, q_ref, k_ref, v_ref, out_hbm, out_ref, sems, *, block,
):
    rows, width = q_ref.shape
    length = length_ref[0]
    copies = []
    for step, first in enumerate(range(0, rows, block)):
        keys = first + block
        query_at = lax.broadcasted_iota(jnp.int32, (block, keys), 0) + first
        key_at = lax.broadcasted_iota(jnp.int32, (block, keys), 1)
        allowed = (key_at <= query_at) & (key_at < length)
        distance = (query_at - key_at).astype(F32)
        for h in range(width // HD):
            cols = slice(h * HD, (h + 1) * HD)
            scores = dot(q_ref[first:keys, cols], k_ref[:keys, cols], ((1,), (1,))) * SCALE
            scores = jnp.where(allowed, scores - head_slope(width // HD, h) * distance, MASKED)
            terms = jnp.exp2(scores - jnp.max(scores, axis=1, keepdims=True))
            weights = (terms / jnp.sum(terms, axis=1, keepdims=True)).astype(BF16)
            out_ref[first:keys, cols] = dot(weights, v_ref[:keys, cols], ((1,), (0,))).astype(BF16)
        for member in range(out_hbm.shape[0]):
            lower = member // 2 % 2 == 0
            if lower and step == 0:
                here, there = slice(0, block), slice(0, block)
            elif lower:
                here, there = slice(block, block + 8), slice(block, block + 8)
            elif step == 1:
                here, there = slice(block, rows), slice(0, block)
            else:
                continue
            copy = pltpu.make_async_copy(out_ref.at[here], out_hbm.at[member, there], sems.at[step, member])
            copy.start()
            copies.append(copy)
    for copy in copies:
        copy.wait()


def prompt(length, q, k, v, members):
    rows, width = q.shape
    block = rows // 2
    return pl.pallas_call(
        functools.partial(prompt_kernel, block=block),
        name="prompt",
        compiler_params=pltpu.CompilerParams(vmem_limit_bytes=ROOM),
        out_shape=placed((members, block + 8, width), BF16),
        in_specs=[SMEM, VMEM, VMEM, VMEM],
        out_specs=HBM,
        scratch_shapes=[
            pltpu.VMEM((rows, width), BF16),
            pltpu.SemaphoreType.DMA((rows // block, members)),
        ],
    )(length, near(q), near(k), near(v))


def insert_kernel(stay_ref, come_ref, given, rows_hbm, tile, sems):
    del given
    row = lax.broadcasted_iota(jnp.int32, tile.shape, 0)
    come = come_ref[0, 0, WIN:].astype(F32)[SPAN - WIN : SPAN - WIN + 1]
    tile[...] = jnp.where(row == 0, stay_ref[...].astype(F32), jnp.where(row == 1, come, 0.0)).astype(BF16)
    members, rows, _ = rows_hbm.shape
    copies = [
        pltpu.make_async_copy(tile, rows_hbm.at[member, pl.ds(rows - 8, 8)], sems.at[member])
        for member in range(members)
        if member // 2 % 2 == 1
    ]
    for copy in copies:
        copy.start()
    for copy in copies:
        copy.wait()


def insert(stay_row, come, rows):
    members, _, width = rows.shape
    return pl.pallas_call(
        insert_kernel,
        name="insert",
        compiler_params=pltpu.CompilerParams(vmem_limit_bytes=ROOM),
        out_shape=placed(rows.shape, rows.dtype),
        in_specs=[VMEM, VMEM, HBM],
        out_specs=HBM,
        scratch_shapes=[pltpu.VMEM((8, width), BF16), pltpu.SemaphoreType.DMA((members,))],
        input_output_aliases={2: 0},
    )(stay_row, near(come), far(rows))


def project_kernel(
    x_ref, w_ref, packed_ref, swapped_ref, bias_ref, residual_hbm,
    own_hbm, pair_hbm, stats_ref, residual_ref, own_ref, pair_ref, sems,
):
    residual_copy = pltpu.make_async_copy(residual_hbm, residual_ref, sems.at[0])
    residual_copy.start()
    sources, rows, width = x_ref.shape
    part = sources // 2
    core, side = core_of(), side_of()
    near_half, far_half = core * part, (1 - core) * part
    blocks = [slice(start, min(start + BLOCK, rows)) for start in range(0, rows, BLOCK)]
    for at in blocks:
        pair_ref[at] = sum(
            dot(x_ref[near_half + s, at], packed_ref[s * width : (s + 1) * width], ((1,), (0,)))
            + dot(x_ref[far_half + s, at], swapped_ref[s * width : (s + 1) * width], ((1,), (0,)))
            for s in range(part)
        )
        own_ref[at] = sum(
            dot(x_ref[s, at], w_ref[s * width : (s + 1) * width], ((1,), (0,))) for s in range(sources)
        )
    residual_copy.wait()
    extra = part * width
    pair_bias = packed_ref[extra + rows :].astype(F32)
    pair_bias = pair_bias[0:1] + pair_bias[1:2]
    copies = []
    for step, at in enumerate(blocks):
        size = at.stop - at.start
        upper = residual_ref[at.start + rows - 8 : min(at.stop + rows - 8, residual_ref.shape[0])].astype(F32)
        if upper.shape[0] < size:
            upper = jnp.concatenate([upper, jnp.zeros((size - upper.shape[0], width), F32)], axis=0)
        own = own_ref[at] + bias_ref[...] + jnp.where(side == 0, residual_ref[at].astype(F32), upper)
        pair = pair_ref[at] + pair_bias + packed_ref[extra + at.start : extra + at.stop].astype(F32)
        own_ref[at] = own
        pair_ref[at] = pair
        for k, (source, target) in enumerate(((own_ref, own_hbm), (pair_ref, pair_hbm))):
            copy = pltpu.make_async_copy(source.at[at], target.at[at], sems.at[1 + 2 * step + k])
            copy.start()
            copies.append(copy)
        mean = jnp.sum(own + pair, axis=1, keepdims=True) * (0.5 / width)
        own_centered, pair_centered = own - mean, pair - mean
        spread = jnp.sum(
            own_centered * own_centered + pair_centered * pair_centered, axis=1, keepdims=True
        )
        lane = lax.broadcasted_iota(jnp.int32, (size, HD), 1)
        table = jnp.where(lane == 0, mean, jnp.where(lane == 1, spread, 0.0))
        stats = table.T[:2]
        for member in range(stats_ref.shape[0]):
            stats_ref[member, :, at] = stats
    for copy in copies:
        copy.wait()


def project(gathered, weight, packed, swapped, bias, residual):
    sources, rows, width = gathered.shape
    steps = -(-rows // BLOCK)
    return pl.pallas_call(
        project_kernel,
        name="project",
        compiler_params=pltpu.CompilerParams(vmem_limit_bytes=ROOM),
        out_shape=(
            placed((rows, width), F32),
            placed((rows, width), F32),
            placed((sources, 2, rows), F32),
        ),
        in_specs=[VMEM] * 5 + [HBM],
        out_specs=(HBM, HBM, VMEM),
        scratch_shapes=[
            pltpu.VMEM(residual.shape, BF16),
            pltpu.VMEM((rows, width), F32),
            pltpu.VMEM((rows, width), F32),
            pltpu.SemaphoreType.DMA((1 + 2 * steps,)),
        ],
    )(near(gathered), near(weight), near(packed), near(swapped), bias, far(residual))


def tables_kernel(stats_ref, out_ref, *, width):
    members, _, rows = stats_ref.shape
    parts = members // 2
    row = lax.broadcasted_iota(jnp.int32, (8, rows), 0)
    for half in range(2):
        sources = [s for s in range(members) if s // 2 % 2 == half]
        means = [stats_ref[s, 0:1, :] for s in sources]
        mean = sum(means) * (1.0 / parts)
        spread = sum(
            stats_ref[s, 1:2, :] + (2 * width) * ((part - mean) * (part - mean))
            for s, part in zip(sources, means)
        )
        scale = lax.rsqrt(spread * (1.0 / (members * width)) + EPSILON)
        out_ref[half] = jnp.where(row == 0, mean, jnp.where(row == 1, scale, 0.0))


def tables(stats, width):
    return pl.pallas_call(
        functools.partial(tables_kernel, width=width),
        name="tables",
        cost_estimate=pl.CostEstimate(flops=8 * 10**9, bytes_accessed=2**20, transcendentals=0),
        compiler_params=pltpu.CompilerParams(vmem_limit_bytes=ROOM),
        out_shape=kept((2, 8, stats.shape[2]), F32),
        in_specs=[VMEM],
        out_specs=VMEM,
    )(near(stats))


def norm_kernel(
    tables_ref, own_hbm, come_ref, gain_ref, shift_ref, hidden_ref, normed_ref, own_ref, sem,
):
    copy = pltpu.make_async_copy(own_hbm, own_ref, sem)
    copy.start()
    copy.wait()
    rows, width = own_ref.shape
    side = side_of()
    total = hidden_ref.shape[0]
    for half in range(2):
        first = half * (rows - 8)
        used = rows - 8 if half == 0 else total - first
        for start in range(0, used, BLOCK):
            at = slice(start, min(start + BLOCK, used))
            columns = tables_ref[half, :, at].T
            own, come = own_ref[at], come_ref[at]
            stream = jnp.where(side == half, own, come)
            to = slice(first + at.start, first + at.stop)
            hidden_ref[to] = stream.astype(BF16)
            normed_ref[to] = (
                (stream - columns[:, 0:1]) * columns[:, 1:2] * gain_ref[...] + shift_ref[...]
            ).astype(BF16)


def norm(scales, own, come, gain, shift, rows):
    out = jax.ShapeDtypeStruct((rows, own.shape[1]), BF16)
    return pl.pallas_call(
        norm_kernel,
        name="norm",
        compiler_params=pltpu.CompilerParams(vmem_limit_bytes=ROOM),
        out_shape=(out, out),
        in_specs=[VMEM, HBM, VMEM, VMEM, VMEM],
        out_specs=(VMEM, VMEM),
        scratch_shapes=[pltpu.VMEM(own.shape, F32), pltpu.SemaphoreType.DMA],
    )(near(scales), far(own), near(come), gain, shift)


def to_partner(block):
    count = lax.axis_size("rep")
    return lax.ppermute(block, "rep", [(i, (i + count // 2) % count) for i in range(count)])


def to_pair(block):
    return lax.ppermute(block, "tp", [(i, i ^ 2) for i in range(lax.axis_size("tp"))])


def to_sibling(block):
    return lax.ppermute(block, "rep", [(i, i ^ 1) for i in range(lax.axis_size("rep"))])


def exchange(blocks):
    return lax.all_to_all(blocks, "tp", 0, 0)


def after(values, other):
    return lax.optimization_barrier((values, other))[0]


def on_device(
    prompt_q, prompt_k, prompt_v, prompt_len, cache_keys, cache_values, new_q, new_k, new_v,
    cache_len, moving, out_weight, out_bias, residual, ln_gain, ln_shift,
):
    window, stay_row, packed = decode(
        moving, cache_len, new_q, new_k, new_v, cache_keys, cache_values, out_weight, residual, out_bias[None]
    )
    come = with_layout_constraint(to_partner(window), Layout((0, 1, 2, 3)))
    packed = to_pair(packed)
    swapped = to_sibling(packed)
    mixed = prompt(prompt_len, prompt_q, prompt_k, prompt_v, lax.axis_size("tp"))
    mixed = insert(stay_row, come, mixed)
    by_row = with_layout_constraint(jnp.transpose(come[:, :, :SPAN], (0, 2, 1, 3)), Layout((0, 1, 2, 3)))
    gathered, by_row = lax.optimization_barrier((exchange(mixed), by_row))
    moved_window = jnp.transpose(by_row, (0, 2, 1, 3))
    own, pair, stats = project(
        gathered, out_weight, packed, swapped, out_bias[None], residual
    )
    scales = tables(exchange(stats), own.shape[1])
    hidden_out, normed = norm(
        scales, own, to_pair(pair), ln_gain[None], ln_shift[None], residual.shape[0]
    )
    return (hidden_out, normed, moved_window)


def solution(mesh):
    in_specs = (
        P("rep", "tp"), P("rep", "tp"), P("rep", "tp"), P("rep"),
        P("rep", None, "tp"), P("rep", None, "tp"),
        P("rep", "tp"), P("rep", "tp"), P("rep", "tp"),
        P(), P(), P(None, "tp"), P("tp"), P("rep", "tp"), P("tp"), P("tp"),
    )
    out_specs = (P("rep", "tp"), P("rep", "tp"), P("rep", None, None, "tp"))
    return jax.shard_map(
        on_device, mesh=mesh, in_specs=in_specs, out_specs=out_specs, check_vma=False
    )
```
